128 devices in a mesh: ra: 16 (over x, y_hi, core), dec: 8 (over z, y_lo).
Axes of the slice: x: 4, y: 4 (y_hi: 2, y_lo: 2; y = y_hi * 2 + y_lo), z: 4, core: 2. Of those that a mesh axis runs over, the one named last changes fastest.
Arguments:
- log_flux: float32 [5, 32768], P(None, ('ra', 'dec')), may hold values from 5.5 to 9.5
- position: float32 [2, 32768], P(None, ('ra', 'dec')), may hold values from 0 to 640
- log_width: float32 [32768], P(('ra', 'dec')), may hold values from -3.5 to -0.5
- owner_tile: int32 [32768, 1], P(('ra', 'dec')), may hold values from 0 to 127; in each aligned block of 256 rows (0 to 255, 256 to 511, ...) at most 4 rows name the same one
- sky_level: float32 [16, 8, 5], P('ra', 'dec'), may hold values from 0.5 to 4
- counts: int32 [5, 10240, 5120], P(None, 'ra', 'dec'), may hold values from 0 to 7
Outputs:
- gradient: float32 [8, 32768], P(None, ('ra', 'dec'))
The draws below stay inside these ranges and needn't reach their ends.
Inputs may be any that keep to these rules, and one draw needn't show every extreme that they name: `owner_tile`: in each aligned block of 256 catalog rows (the rows of one device) no tile is named more than 4 times, a bound that some block reaches.
All inputs are finite; a program needn't handle non-finite values.
Results may differ from the reference program's by a relative error of at most 0.00095.
Values may be sent and summed in bfloat16 or wider, within the bound.
A program may use at most 128 MiB of HBM per device.

```python
import math
import jax
import jax.numpy as jnp
import numpy as np
from jax import lax

BANDS = 5
TILE = 640
MARGIN = 128
CAT_DEV = 256
TILES = 128
CAP = 4
SLOTS = 512
CANVAS = 896
CAT = 32768
SKY_RA = 10240
SKY_DEC = 5120
N_RA = 16
N_DEC = 8


def draw_position(key, part):
    uniform_part = jax.random.uniform(jax.random.fold_in(key, 11), (2, CAT), jnp.float32)
    centered = 2.0 * uniform_part - 1.0
    power = 0.5
    warped = jnp.where(centered >= 0.0, 1.0, -1.0) * jnp.abs(centered) ** power
    return jnp.clip(0.5 * TILE * (1.0 + warped), 0.0, 1.0 * TILE).astype(jnp.float32)


def draw_counts(key, part):
    top_count = 4 + 6400 * CAT_DEV // (TILE * TILE)
    region_rows = (SKY_RA + MARGIN - 1) // MARGIN
    region_cols = (SKY_DEC + MARGIN - 1) // MARGIN
    phase_rows = jax.random.randint(jax.random.fold_in(key, 21), (BANDS, region_rows, region_cols), 0, 4)
    phase_cols = jax.random.randint(jax.random.fold_in(key, 22), (BANDS, region_rows, region_cols), 0, 4)
    phase_rows = jnp.repeat(jnp.repeat(phase_rows, MARGIN, axis=1), MARGIN, axis=2)[:, :SKY_RA, :SKY_DEC]
    phase_cols = jnp.repeat(jnp.repeat(phase_cols, MARGIN, axis=1), MARGIN, axis=2)[:, :SKY_RA, :SKY_DEC]
    pixel_rows = jnp.arange(SKY_RA, dtype=jnp.int32)[None, :, None]
    pixel_cols = jnp.arange(SKY_DEC, dtype=jnp.int32)[None, None, :]
    bright = ((pixel_rows + phase_rows) % 4 >= 2) | ((pixel_cols + phase_cols) % 4 >= 2)
    noise = jax.random.randint(jax.random.fold_in(key, 23), (BANDS, SKY_RA, SKY_DEC), 0, top_count // 4 + 1)
    return jnp.where(bright, top_count - 1 - noise, noise).astype(jnp.int32)


def levels(key, shape, split, smallest, high):
    def one(dim, blocks):
        heights = jax.random.uniform(jax.random.fold_in(jax.random.fold_in(key, 6), dim), (blocks,), jnp.float32, smallest / len(split), high / len(split))
        return jnp.repeat(jnp.exp(heights), shape[dim] // blocks).reshape((-1,) + (1,) * (len(shape) - dim - 1))

    gain = one(*split[0])
    for cut in split[1:]:
        gain = gain * one(*cut)
    return gain


def routed_block(key, own, number, rows, count, top, bound, lean):
    ranking = jax.random.permutation(key, count)
    crowded, usual = shares(count, rows * top, bound, lean, True), shares(count, rows * top, bound, lean, False)
    places = jnp.arange(count)

    def named(tallies, offset_by):
        used = int((tallies > 0).sum())
        fixed = max(1, used // 4)
        shifted = fixed + (places - fixed + offset_by * (used - fixed)) % max(1, count - fixed)
        return jnp.zeros((count,), jnp.int32).at[ranking[jnp.where(places < fixed, places, shifted)]].set(jnp.asarray(tallies, jnp.int32))

    tallies = jnp.where(number % 4 == 0, named(crowded, number // 4), named(usual, number - number // 4 - 1))
    mixed = jax.random.permutation(jax.random.fold_in(own, 3), count)
    donor, receiver = mixed[0:count // 2 * 2:2], mixed[1:count // 2 * 2:2]
    slack = jnp.minimum(tallies[donor] - 1, bound - tallies[receiver]) // 2
    slack = jnp.where((donor == ranking[0]) | (receiver == ranking[0]) | (tallies[receiver] == 0), 0, jnp.maximum(slack, 0))
    shifted = jax.random.randint(jax.random.fold_in(own, 4), (count // 2,), 0, 1 << 20) % (slack + 1)
    tallies = tallies.at[donor].add(-shifted).at[receiver].add(shifted)
    members = jnp.searchsorted(jnp.cumsum(tallies), jnp.arange(rows * top), side="right").astype(jnp.int32)
    table = members.reshape(top, rows).T
    table = table[jax.random.permutation(jax.random.fold_in(own, 1), rows)]
    offset_by = jax.random.randint(jax.random.fold_in(own, 2), (rows, 1), 0, top)
    return jnp.take_along_axis(table, (jnp.arange(top)[None, :] + offset_by) % top, axis=1)


def shares(number_of, total, limit, skew, full):
    weights = [(1 << 20) // math.isqrt(rank ** skew) + 1 for rank in range(1, number_of + 1)]
    largest = limit if full else min(limit, max(-(-total // number_of), total * weights[0] // sum(weights)))
    least = 1 if total - largest >= number_of - 1 else 0
    holding, surplus = [largest] + [least] * (number_of - 1), total - largest - least * (number_of - 1)
    while surplus > 0:
        movable = [i for i in range(1, number_of) if holding[i] < largest] or [i for i in range(1, number_of) if holding[i] < limit]
        pool, left = sum([weights[i] for i in movable]), surplus
        for i in movable:
            more = min(limit - holding[i], max(1, left * weights[i] // pool), surplus)
            holding[i] = holding[i] + more
            surplus = surplus - more
    return np.array(holding)


def setup_inputs(seed: int = 0) -> dict:
    key_of = jax.random.split(jax.random.key(seed), 7)
    log_flux = jnp.clip(5.5 + 4.0 * jax.random.uniform(key_of[0], (BANDS, CAT), jnp.float32) ** levels(key_of[0], (BANDS, CAT), ((1, 128),), -0.2, 0.2), 5.5, 9.5)
    position = draw_position(jax.random.fold_in(key_of[6], 71), 0)
    log_width = jnp.clip(-3.5 + 3.0 * jax.random.uniform(key_of[2], (CAT,), jnp.float32) ** levels(key_of[2], (CAT,), ((0, 128),), -0.2, 0.2), -3.5, -0.5)
    owner_tile_keys = jax.random.split(jax.random.fold_in(key_of[3], 1), CAT // CAT_DEV)
    owner_tile_turns = jax.random.permutation(jax.random.fold_in(key_of[3], 3), CAT // CAT_DEV)
    owner_tile = jax.vmap(lambda own, number: routed_block(jax.random.fold_in(key_of[3], 2), own, number, CAT_DEV, TILES, 1, CAP, 2))(owner_tile_keys, owner_tile_turns).reshape((CAT, 1))
    sky_level = jnp.clip(jnp.exp(math.log(4.0) - 2.0794415 * jax.random.uniform(key_of[4], (N_RA, N_DEC, BANDS), jnp.float32) ** levels(key_of[4], (N_RA, N_DEC, BANDS), ((0, 16), (1, 8)), -0.2, 0.2)), 0.5, 4.0)
    counts = draw_counts(jax.random.fold_in(key_of[6], 71), 0)
    return dict(log_flux=log_flux, position=position, log_width=log_width, owner_tile=owner_tile, sky_level=sky_level, counts=counts)


def profiles(center, log_width):
    coords = jnp.arange(CANVAS, dtype=jnp.float32) - MARGIN + 0.5
    sigma = MARGIN * jnp.exp(log_width)
    offset = (coords[:, None] - center[None, :]) / sigma[None, :]
    shape = jnp.exp(-0.5 * offset * offset) / (math.sqrt(2.0 * math.pi) * sigma[None, :])
    return (shape, offset, sigma)

def render(arrived):
    flux_values = arrived[8][None, :] * jnp.exp(arrived[0:5])
    row_prof, _, _ = profiles(arrived[5], arrived[7])
    col_prof, _, _ = profiles(arrived[6], arrived[7])
    scaled = (row_prof[None, :, :] * flux_values[:, None, :]).astype(jnp.bfloat16)
    col_bf = col_prof.astype(jnp.bfloat16)
    canvas = jnp.einsum('bis,js->bij', scaled.astype(jnp.float32), col_bf.astype(jnp.float32))
    return canvas.astype(jnp.bfloat16)

def tile_grads(arrived, weight_canvas):
    flux_values = arrived[8][None, :] * jnp.exp(arrived[0:5])
    row_prof, row_off, sigma = profiles(arrived[5], arrived[7])
    col_prof, col_off, _ = profiles(arrived[6], arrived[7])
    row_bf = row_prof.astype(jnp.bfloat16).astype(jnp.float32)
    col_bf = col_prof.astype(jnp.bfloat16).astype(jnp.float32)
    wfloat = weight_canvas.astype(jnp.float32)
    along_rows = jnp.einsum('bij,js->bis', wfloat, col_bf)
    along_cols = jnp.einsum('bij,is->bjs', wfloat, row_bf)
    flux_grad = flux_values * lax.optimization_barrier(jnp.sum(row_bf[None, :, :] * along_rows, axis=1))
    row_total = lax.optimization_barrier(jnp.sum(flux_values[:, None, :] * along_rows, axis=0))
    col_total = lax.optimization_barrier(jnp.sum(flux_values[:, None, :] * along_cols, axis=0))
    row_grad = lax.optimization_barrier(jnp.sum(row_prof * row_off / sigma[None, :] * row_total, axis=0))
    col_grad = lax.optimization_barrier(jnp.sum(col_prof * col_off / sigma[None, :] * col_total, axis=0))
    width_grad = lax.optimization_barrier(jnp.sum(row_prof * (row_off * row_off - 1.0) * row_total, axis=0)) + lax.optimization_barrier(jnp.sum(col_prof * (col_off * col_off - 1.0) * col_total, axis=0))
    return jnp.concatenate([flux_grad, row_grad[None], col_grad[None], width_grad[None]], axis=0)

def reference(log_flux, position, log_width, owner_tile, sky_level, counts):
    params = jnp.concatenate([log_flux, position, log_width[None, :], jnp.ones((1, CAT), jnp.float32)], axis=0)
    target_tile = owner_tile[:, 0]
    blocks = target_tile.reshape(TILES, CAT_DEV)
    matches = blocks[:, None, :] == blocks[:, :, None]
    order = jnp.arange(CAT_DEV, dtype=jnp.int32)
    earlier = order[None, :] < order[:, None]
    rank_in = lax.optimization_barrier(jnp.sum((matches & earlier[None]).astype(jnp.int32), axis=2)).reshape(CAT)
    slot_of = jnp.arange(CAT, dtype=jnp.int32) // CAT_DEV * CAP + rank_in
    arrived = jnp.zeros((TILES, 9, SLOTS), jnp.float32).at[target_tile, :, slot_of].set(params.T)

    def add_tile(padded, tile_index):
        ra_index = (tile_index // N_DEC).astype(jnp.int32)
        dec_index = (tile_index % N_DEC).astype(jnp.int32)
        canvas = render(arrived[tile_index])
        piece = lax.optimization_barrier(canvas).astype(jnp.float32)
        starts = (jnp.int32(0), ra_index * TILE, dec_index * TILE)
        region = lax.dynamic_slice(padded, starts, (BANDS, CANVAS, CANVAS))
        return (lax.dynamic_update_slice(padded, region + piece, starts), None)
    padded, _ = lax.scan(add_tile, jnp.zeros((BANDS, SKY_RA + 2 * MARGIN, SKY_DEC + 2 * MARGIN), jnp.float32), jnp.arange(TILES, dtype=jnp.int32))
    sky_model = padded[:, MARGIN:MARGIN + SKY_RA, MARGIN:MARGIN + SKY_DEC].reshape(BANDS, N_RA, TILE, N_DEC, TILE)
    background = jnp.transpose(sky_level, (2, 0, 1))[:, :, None, :, None]
    intensity = (sky_model + background).reshape(BANDS, SKY_RA, SKY_DEC)
    weights = (counts.astype(jnp.float32) / intensity - 1.0).astype(jnp.bfloat16)
    wpadded = jnp.pad(weights, ((0, 0), (MARGIN, MARGIN), (MARGIN, MARGIN)))

    def one_tile(tile_index):
        ra_index = (tile_index // N_DEC).astype(jnp.int32)
        dec_index = (tile_index % N_DEC).astype(jnp.int32)
        window = lax.dynamic_slice(wpadded, (jnp.int32(0), ra_index * TILE, dec_index * TILE), (BANDS, CANVAS, CANVAS))
        return tile_grads(arrived[tile_index], window)
    slot_grad = lax.map(one_tile, jnp.arange(TILES, dtype=jnp.int32))
    return slot_grad[target_tile, :, slot_of].T
```

```python
import functools
import math

import jax
import jax.numpy as jnp
from jax import lax
from jax.experimental import pallas as pl
from jax.experimental.pallas import tpu as pltpu
from jax.sharding import PartitionSpec as P

F32 = jnp.float32
BF16 = jnp.bfloat16
MESH = pl.DeviceIdType.MESH
VMEM = pl.BlockSpec(memory_space=pltpu.VMEM)

EDGE = 128
RANKS = 4
LANES = 128
HALF_LOG2E = 0.5 * math.log2(math.e)
ROOT_2PI = math.sqrt(2.0 * math.pi)


def split3(x):
    hi = x.astype(BF16)
    rest = x - hi.astype(F32)
    mid = rest.astype(BF16)
    lo = (rest - mid.astype(F32)).astype(BF16)
    return hi, mid, lo


def dot_tt(a, b):
    return lax.dot_general(a, b, (((1,), (1,)), ((), ())), preferred_element_type=F32)


def dot_nn(a, b):
    return lax.dot_general(a, b, (((1,), (0,)), ((), ())), preferred_element_type=F32)


def ranks_of(tile):
    rows = tile.shape[1]
    names = lax.broadcasted_iota(jnp.int32, (LANES, rows), 0)
    onehot = names == tile
    earlier = lax.broadcasted_iota(jnp.int32, (rows, rows), 0) < lax.broadcasted_iota(
        jnp.int32, (rows, rows), 1
    )
    before = dot_nn(
        jnp.where(onehot, 1.0, 0.0).astype(BF16), jnp.where(earlier, 1.0, 0.0).astype(BF16)
    )
    rank = jnp.sum(jnp.where(onehot, before, 0.0), axis=0, keepdims=True)
    return names, rank


def barrier_signal(na, nd, a, d):
    barrier = pltpu.get_barrier_semaphore()
    for off in range(1, na):
        pl.semaphore_signal(
            barrier, inc=1, device_id=(lax.rem(a + off, na), d), device_id_type=MESH
        )
    for off in range(1, nd):
        pl.semaphore_signal(
            barrier, inc=1, device_id=(a, lax.rem(d + off, nd)), device_id_type=MESH
        )


def barrier_wait(na, nd):
    pl.semaphore_wait(pltpu.get_barrier_semaphore(), na - 1 + nd - 1)


def route_kernel(
    na, nd, flux_ref, pos_ref, width_ref, tile_ref, out_ref,
    params, first, got1, stage, got2, send1, recv1, send2, recv2,
):
    a, d = lax.axis_index("ra"), lax.axis_index("dec")
    barrier_signal(na, nd, a, d)
    params[0:5, :] = jnp.exp(flux_ref[...])
    params[5:7, :] = pos_ref[...]
    params[7:8, :] = width_ref[...]
    tile = tile_ref[...]
    rows = tile.shape[1]
    names, rank = ranks_of(tile)
    block = params[...]
    ranked = jnp.concatenate(
        [jnp.where(rank == float(k), block, 0.0) for k in range(RANKS)], axis=0
    )
    gap = jnp.zeros((LANES - ranked.shape[0] * 3, rows), BF16)
    none = jnp.zeros(ranked.shape, BF16)
    pieces = split3(ranked)
    total = None
    for n in range(3):
        hot = jnp.where(names + (n - 1) * nd == tile, 1.0, 0.0).astype(BF16)
        for piece in pieces:
            rhs = jnp.concatenate([piece if m == n else none for m in range(3)] + [gap], axis=0)
            term = dot_tt(hot, rhs)
            total = term if total is None else total + term
    first[...] = total.reshape(na, nd, LANES)
    barrier_wait(na, nd)

    sends = []
    for off in range(1, na):
        peer = lax.rem(a + off, na)
        copy = pltpu.make_async_remote_copy(
            src_ref=first.at[peer], dst_ref=got1.at[a], send_sem=send1.at[off],
            recv_sem=recv1.at[a], device_id=(peer, d), device_id_type=MESH,
        )
        copy.start()
        sends.append(copy)
    got1[a] = first[a]
    stage[0] = jnp.zeros((na, LANES), F32)
    stage[nd + 1] = jnp.zeros((na, LANES), F32)
    for off in range(1, na):
        peer = lax.rem(a + off, na)
        pltpu.make_async_remote_copy(
            src_ref=got1.at[peer], dst_ref=got1.at[peer], send_sem=send1.at[off],
            recv_sem=recv1.at[peer], device_id=(peer, d), device_id_type=MESH,
        ).wait_recv()
    for col in range(nd):
        stage[col + 1] = got1[:, col, :]
    for off in range(1, nd):
        peer = lax.rem(d + off, nd)
        copy = pltpu.make_async_remote_copy(
            src_ref=stage.at[pl.ds(peer, 3)], dst_ref=got2.at[d], send_sem=send2.at[off],
            recv_sem=recv2.at[d], device_id=(a, peer), device_id_type=MESH,
        )
        copy.start()
        sends.append(copy)
    got2[d] = stage[pl.ds(d, 3)]
    for off in range(1, nd):
        peer = lax.rem(d + off, nd)
        pltpu.make_async_remote_copy(
            src_ref=stage.at[pl.ds(peer, 3)], dst_ref=got2.at[peer], send_sem=send2.at[off],
            recv_sem=recv2.at[peer], device_id=(a, peer), device_id_type=MESH,
        ).wait_recv()
    for n in range(3):
        out_ref[n] = got2[:, n].reshape(na * nd, LANES).T
    for copy in sends:
        copy.wait_send()


def return_kernel(
    na, nd, grad_ref, tile_ref, out_ref,
    first, got1, stage, got2, send1, recv1, send2, recv2,
):
    a, d = lax.axis_index("ra"), lax.axis_index("dec")
    barrier_signal(na, nd, a, d)
    for n in range(3):
        first[:, n] = grad_ref[n].T.reshape(nd, na, LANES)
    got1[nd] = jnp.zeros(got1.shape[1:], F32)
    got1[nd + 1] = jnp.zeros(got1.shape[1:], F32)
    got2[na] = jnp.zeros(got2.shape[1:], F32)
    got2[na + 1] = jnp.zeros(got2.shape[1:], F32)
    tile = tile_ref[...]
    names, rank = ranks_of(tile)
    hot = jnp.where(names == tile, 1.0, 0.0).astype(BF16)
    barrier_wait(na, nd)

    sends = []
    for off in range(1, nd):
        peer = lax.rem(d + off, nd)
        copy = pltpu.make_async_remote_copy(
            src_ref=first.at[peer], dst_ref=got1.at[d], send_sem=send1.at[off],
            recv_sem=recv1.at[d], device_id=(a, peer), device_id_type=MESH,
        )
        copy.start()
        sends.append(copy)
    got1[d] = first[d]
    for off in range(1, nd):
        peer = lax.rem(d + off, nd)
        pltpu.make_async_remote_copy(
            src_ref=first.at[peer], dst_ref=got1.at[peer], send_sem=send1.at[off],
            recv_sem=recv1.at[peer], device_id=(a, peer), device_id_type=MESH,
        ).wait_recv()
    for col in range(nd):
        after, before = (col + 1 if col + 1 < nd else nd), (col - 1 if col else nd + 1)
        stage[:, col, :] = got1[after, 0] + got1[col, 1] + got1[before, 2]
    for off in range(1, na):
        peer = lax.rem(a + off, na)
        copy = pltpu.make_async_remote_copy(
            src_ref=stage.at[peer], dst_ref=got2.at[a], send_sem=send2.at[off],
            recv_sem=recv2.at[a], device_id=(peer, d), device_id_type=MESH,
        )
        copy.start()
        sends.append(copy)
    got2[a] = stage[a]
    for off in range(1, na):
        peer = lax.rem(a + off, na)
        pltpu.make_async_remote_copy(
            src_ref=stage.at[peer], dst_ref=got2.at[peer], send_sem=send2.at[off],
            recv_sem=recv2.at[peer], device_id=(peer, d), device_id_type=MESH,
        ).wait_recv()
    mine = got2[0:na].reshape(na * nd, LANES)
    none = jnp.zeros((nd, LANES), F32)
    later = jnp.concatenate([mine[nd:], none], axis=0)
    sooner = jnp.concatenate([none, mine[:-nd]], axis=0)
    held, width = mine.T, 8 * RANKS
    slots = (
        later.T[0:width] + held[width : 2 * width] + sooner.T[2 * width : 3 * width]
    )
    rows = None
    for piece in split3(slots):
        term = dot_nn(piece, hot)
        rows = term if rows is None else rows + term
    total = None
    for k in range(RANKS):
        term = jnp.where(rank == float(k), rows[8 * k : 8 * k + 8], 0.0)
        total = term if total is None else total + term
    out_ref[...] = total
    for copy in sends:
        copy.wait_send()


CORNERS = ((-1, -1), (-1, 1), (1, -1), (1, 1))
SIDES = ((-1, 0), (1, 0), (0, -1), (0, 1))
GROUPS = CORNERS + SIDES + ((0, 0),)
BANDS = 5
STEP = 64
OUTS = BANDS + 6


def compute_kernel(
    side, src_ref, sky_ref, counts_ref, out_ref,
    counts, weights, turned, prof_i, prof_j, low_i, low_j, scaled,
    rim_top, rim_bottom, rim_left, rim_right, sums, count_sem,
):
    slots = RANKS * LANES

    def copy_in(b):
        return pltpu.make_async_copy(counts_ref.at[b], counts.at[b], count_sem.at[b])

    for b in range(BANDS):
        copy_in(b).start()
    sums[...] = jnp.zeros_like(sums)
    index = {group: n for n, group in enumerate(GROUPS)}

    def source(group, k, row):
        dr, dc = group
        start = (dr + 1) * 8 * RANKS + k * 8 + row
        return src_ref[dc + 1, start : start + 1, :]

    def span(step):
        if step == 0:
            return 0, side
        return (0, EDGE) if step < 0 else (side - EDGE, EDGE)

    def make_profile(group, axis, f32_ref, low_ref, scaled_ref):
        first, count = span(group[axis])
        base = first + 0.5 - group[axis] * side
        iota = lax.broadcasted_iota(jnp.int32, (STEP, LANES), 0).astype(F32)
        for k in range(RANKS):
            lanes = slice(k * LANES, (k + 1) * LANES)
            center = source(group, k, 5 + axis)
            inverse = 1.0 / (float(EDGE) * jnp.exp(source(group, k, 7)))
            factor = -HALF_LOG2E * inverse * inverse
            norm = inverse * (1.0 / ROOT_2PI)
            flux = [source(group, k, b) for b in range(BANDS)] if scaled_ref is not None else []

            def body(step, carry):
                start = pl.multiple_of(step * STEP, STEP)
                off = iota + (base + start.astype(F32)) - center
                prof = jnp.exp2(off * factor * off) * norm
                rows = pl.ds(start, STEP)
                f32_ref[rows, lanes] = prof
                if low_ref is not None:
                    low_ref[rows, lanes] = prof.astype(BF16)
                for b, f in enumerate(flux):
                    into = pl.ds(pl.multiple_of(b * count + step * STEP, STEP), STEP)
                    scaled_ref[into, lanes] = (prof * f).astype(BF16)
                return carry

            lax.fori_loop(0, count // STEP, body, 0)

    def rounded(x):
        return x.astype(BF16).astype(F32)

    rims_ij = {-1: rim_top, 1: rim_bottom}
    rims_ji = {-1: rim_left, 1: rim_right}
    for group in SIDES + CORNERS:
        n = index[group]
        dr, dc = group
        if dr:
            make_profile(group, 0, prof_i[n], None, scaled[n])
            make_profile(group, 1, prof_j[n], low_j[n], None)
            part = rounded(dot_tt(scaled[n][...], low_j[n][...]))
            part = part.reshape(BANDS, EDGE, part.shape[1])
            if dc == 0:
                rims_ij[dr][...] = part
            else:
                start = 0 if dc < 0 else side - EDGE
                rims_ij[dr][:, :, start : start + EDGE] += part
        else:
            make_profile(group, 0, prof_i[n], low_i[n], None)
            make_profile(group, 1, prof_j[n], None, scaled[n])
            rims_ji[dc][...] = rounded(dot_tt(low_i[n][...], scaled[n][...]))

    own = index[(0, 0)]
    make_profile((0, 0), 0, prof_i[own], low_i[own], scaled[own])
    make_profile((0, 0), 1, prof_j[own], low_j[own], None)

    for b in range(BANDS):
        model = rounded(dot_tt(scaled[own][b * side : (b + 1) * side, :], low_j[own][...]))
        copy_in(b).wait()
        level = sky_ref[0, 0, b]
        for chunk in range(side // EDGE):
            rows = slice(chunk * EDGE, (chunk + 1) * EDGE)
            for other in range(side // EDGE):
                cols = slice(other * EDGE, (other + 1) * EDGE)
                part = model[rows, cols] + level
                if other == 0:
                    part = part + rim_left[rows, b * EDGE : (b + 1) * EDGE]
                if other == side // EDGE - 1:
                    part = part + rim_right[rows, b * EDGE : (b + 1) * EDGE]
                if chunk == 0:
                    part = part + rim_top[b, :, cols]
                if chunk == side // EDGE - 1:
                    part = part + rim_bottom[b, :, cols]
                ratio = counts[b, rows, cols].astype(F32) / part - 1.0
                low = ratio.astype(BF16)
                weights[b, rows, cols] = low
                turned[cols, b * side + chunk * EDGE : b * side + (chunk + 1) * EDGE] = low.T

    def fold(x):
        return jnp.sum(x.reshape(x.shape[0] // 8, 8, x.shape[1]), axis=0)

    def moments(group, axis, k, start, total, prof, base):
        n = index[group]
        iota = lax.broadcasted_iota(jnp.int32, total.shape, 0).astype(F32)
        off = iota + (base + start) - source(group, k, 5 + axis)
        zeroth = prof * total
        once = zeroth * off
        twice = once * off
        at = BANDS + 3 * axis
        sums[n, k, at] += fold(zeroth)
        sums[n, k, at + 1] += fold(once)
        sums[n, k, at + 2] += fold(twice)

    def per_band(group, axis, lhs, rhs, prof_ref, rows, start):
        n = index[group]
        base = span(group[axis])[0] + 0.5 - group[axis] * side
        for pair in range(RANKS // 2):
            wide = slice(pair * 2 * LANES, (pair + 1) * 2 * LANES)
            along = dot_nn(lhs, rhs[:, wide])
            for k in (2 * pair, 2 * pair + 1):
                lanes = slice((k - 2 * pair) * LANES, (k - 2 * pair + 1) * LANES)
                prof = prof_ref[rows, k * LANES : (k + 1) * LANES]
                low = rounded(prof)
                total = None
                for b in range(BANDS):
                    band = along[b * EDGE : (b + 1) * EDGE, lanes]
                    sums[n, k, b] += fold(low * band)
                    term = source(group, k, b) * band
                    total = term if total is None else total + term
                moments(group, axis, k, start, total, prof, base)

    def all_bands(group, axis, lhs, scaled_ref, prof_ref):
        base = span(group[axis])[0] + 0.5 - group[axis] * side
        for pair in range(RANKS // 2):
            wide = slice(pair * 2 * LANES, (pair + 1) * 2 * LANES)
            along = dot_nn(lhs, scaled_ref[:, wide])
            for k in (2 * pair, 2 * pair + 1):
                lanes = slice((k - 2 * pair) * LANES, (k - 2 * pair + 1) * LANES)
                prof = prof_ref[:, k * LANES : (k + 1) * LANES]
                moments(group, axis, k, 0.0, along[:, lanes], prof, base)

    for group in SIDES + CORNERS:
        n = index[group]
        (r0, rn), (c0, cn) = span(group[0]), span(group[1])
        if group[0]:
            lhs = weights[:, r0 : r0 + rn, c0 : c0 + cn].reshape(BANDS * rn, cn)
            per_band(group, 0, lhs, low_j[n], prof_i[n], slice(0, EDGE), 0.0)
            lhs = jnp.concatenate(
                [turned[c0 : c0 + cn, b * side + r0 : b * side + r0 + rn] for b in range(BANDS)],
                axis=1,
            )
            all_bands(group, 1, lhs, scaled[n], prof_j[n])
        else:
            lhs = jnp.concatenate(
                [turned[c0 : c0 + cn, b * side : (b + 1) * side] for b in range(BANDS)], axis=0
            )
            per_band(group, 1, lhs, low_i[n], prof_j[n], slice(0, EDGE), 0.0)
            lhs = jnp.concatenate([weights[b, :, c0 : c0 + cn] for b in range(BANDS)], axis=1)
            all_bands(group, 0, lhs, scaled[n], prof_i[n])

    def own_chunk(chunk, carry):
        start = pl.multiple_of(chunk * EDGE, EDGE)
        lhs = weights[:, pl.ds(start, EDGE), :].reshape(BANDS * EDGE, side)
        per_band(
            (0, 0), 0, lhs, low_j[own], prof_i[own], pl.ds(start, EDGE), start.astype(F32)
        )
        return carry

    lax.fori_loop(0, side // EDGE, own_chunk, 0)
    all_bands((0, 0), 1, turned[...], scaled[own], prof_j[own])

    out_ref[...] = jnp.zeros_like(out_ref)
    for group in GROUPS:
        n, (dr, dc) = index[group], group
        for k in range(RANKS):
            inverse = 1.0 / (float(EDGE) * jnp.exp(source(group, k, 7)))
            square = inverse * inverse

            def total(which):
                return jnp.sum(sums[n, k, which], axis=0, keepdims=True)

            start = (dr + 1) * 8 * RANKS + k * 8
            for b in range(BANDS):
                out_ref[dc + 1, start + b : start + b + 1, :] = source(group, k, b) * total(b)
            zeroth = total(BANDS) + total(BANDS + 3)
            second = total(BANDS + 2) + total(BANDS + 5)
            out_ref[dc + 1, start + 5 : start + 6, :] = total(BANDS + 1) * square
            out_ref[dc + 1, start + 6 : start + 7, :] = total(BANDS + 4) * square
            out_ref[dc + 1, start + 7 : start + 8, :] = second * square - zeroth


def on_device(na, nd, log_flux, position, log_width, owner_tile, sky_level, counts):
    rows = log_flux.shape[1]
    side = counts.shape[1]
    slots = RANKS * LANES
    width = log_width.reshape(1, rows)
    tile = owner_tile.reshape(1, rows)
    dma = pltpu.SemaphoreType.DMA

    routed = pl.pallas_call(
        functools.partial(route_kernel, na, nd),
        out_shape=jax.ShapeDtypeStruct((3, LANES, na * nd), F32),
        in_specs=[VMEM] * 4,
        out_specs=VMEM,
        scratch_shapes=[
            pltpu.VMEM((8, rows), F32),
            pltpu.VMEM((na, nd, LANES), F32),
            pltpu.VMEM((na, nd, LANES), F32),
            pltpu.VMEM((nd + 2, na, LANES), F32),
            pltpu.VMEM((nd, 3, na, LANES), F32),
            dma((na,)), dma((na,)), dma((nd,)), dma((nd,)),
        ],
        compiler_params=pltpu.CompilerParams(collective_id=0, has_side_effects=True),
        name="route",
    )(log_flux, position, width, tile)

    def extent(step):
        return EDGE if step else side

    prof_i = [pltpu.VMEM((extent(g[0]), slots), F32) for g in GROUPS]
    prof_j = [pltpu.VMEM((extent(g[1]), slots), F32) for g in GROUPS]
    low_i = [pltpu.VMEM((extent(g[0]) if g[0] == 0 else 16, slots), BF16) for g in GROUPS]
    low_j = [pltpu.VMEM((extent(g[1]) if g[0] or not g[1] else 16, slots), BF16) for g in GROUPS]
    scaled = [pltpu.VMEM((BANDS * (EDGE if g != (0, 0) else side), slots), BF16) for g in GROUPS]
    partial = pl.pallas_call(
        functools.partial(compute_kernel, side),
        out_shape=jax.ShapeDtypeStruct((3, LANES, na * nd), F32),
        in_specs=[
            VMEM,
            pl.BlockSpec(memory_space=pltpu.SMEM),
            pl.BlockSpec(memory_space=pl.ANY),
        ],
        out_specs=VMEM,
        scratch_shapes=[
            pltpu.VMEM((BANDS, side, side), jnp.int32),
            pltpu.VMEM((BANDS, side, side), BF16),
            pltpu.VMEM((side, BANDS * side), BF16),
            prof_i, prof_j, low_i, low_j, scaled,
            pltpu.VMEM((BANDS, EDGE, side), F32),
            pltpu.VMEM((BANDS, EDGE, side), F32),
            pltpu.VMEM((side, BANDS * EDGE), F32),
            pltpu.VMEM((side, BANDS * EDGE), F32),
            pltpu.VMEM((len(GROUPS), RANKS, OUTS, 8, LANES), F32),
            dma((BANDS,)),
        ],
        compiler_params=pltpu.CompilerParams(vmem_limit_bytes=60 << 20),
        name="compute",
    )(routed, sky_level, counts)

    return pl.pallas_call(
        functools.partial(return_kernel, na, nd),
        out_shape=jax.ShapeDtypeStruct((8, rows), F32),
        in_specs=[VMEM] * 2,
        out_specs=VMEM,
        scratch_shapes=[
            pltpu.VMEM((nd, 3, na, LANES), F32),
            pltpu.VMEM((nd + 2, 3, na, LANES), F32),
            pltpu.VMEM((na, nd, LANES), F32),
            pltpu.VMEM((na + 2, nd, LANES), F32),
            dma((nd,)), dma((nd,)), dma((na,)), dma((na,)),
        ],
        compiler_params=pltpu.CompilerParams(collective_id=1, has_side_effects=True),
        name="give_back",
    )(partial, tile)


def solution(mesh):
    na, nd = mesh.shape["ra"], mesh.shape["dec"]
    in_specs = (
        P(None, ("ra", "dec")),
        P(None, ("ra", "dec")),
        P(("ra", "dec")),
        P(("ra", "dec"), None),
        P("ra", "dec", None),
        P(None, "ra", "dec"),
    )
    return jax.shard_map(
        functools.partial(on_device, na, nd),
        mesh=mesh,
        in_specs=in_specs,
        out_specs=P(None, ("ra", "dec")),
        check_vma=False,
    )
```

```python
import functools
import math

import jax
import jax.numpy as jnp
from jax import lax
from jax.experimental import pallas as pl
from jax.experimental.pallas import tpu as pltpu
from jax.sharding import PartitionSpec as P

F32 = jnp.float32
BF16 = jnp.bfloat16
MESH = pl.DeviceIdType.MESH
VMEM = pl.BlockSpec(memory_space=pltpu.VMEM)

EDGE = 128
RANKS = 4
LANES = 128
HALF_LOG2E = 0.5 * math.log2(math.e)
ROOT_2PI = math.sqrt(2.0 * math.pi)


def split3(x):
    hi = x.astype(BF16)
    rest = x - hi.astype(F32)
    mid = rest.astype(BF16)
    lo = (rest - mid.astype(F32)).astype(BF16)
    return hi, mid, lo


def dot_tt(a, b):
    return lax.dot_general(a, b, (((1,), (1,)), ((), ())), preferred_element_type=F32)


def dot_nn(a, b):
    return lax.dot_general(a, b, (((1,), (0,)), ((), ())), preferred_element_type=F32)


def ranks_of(tile):
    rows = tile.shape[1]
    names = lax.broadcasted_iota(jnp.int32, (LANES, rows), 0)
    onehot = names == tile
    earlier = lax.broadcasted_iota(jnp.int32, (rows, rows), 0) < lax.broadcasted_iota(
        jnp.int32, (rows, rows), 1
    )
    before = dot_nn(
        jnp.where(onehot, 1.0, 0.0).astype(BF16), jnp.where(earlier, 1.0, 0.0).astype(BF16)
    )
    rank = jnp.sum(jnp.where(onehot, before, 0.0), axis=0, keepdims=True)
    return names, rank


def barrier_signal(na, nd, a, d):
    barrier = pltpu.get_barrier_semaphore()
    for off in range(1, na):
        pl.semaphore_signal(
            barrier, inc=1, device_id=(lax.rem(a + off, na), d), device_id_type=MESH
        )
    for off in range(1, nd):
        pl.semaphore_signal(
            barrier, inc=1, device_id=(a, lax.rem(d + off, nd)), device_id_type=MESH
        )


def barrier_wait(na, nd):
    pl.semaphore_wait(pltpu.get_barrier_semaphore(), na - 1 + nd - 1)


def route_kernel(
    na, nd, flux_ref, pos_ref, width_ref, tile_ref, out_ref,
    params, first, got1, stage, got2, send1, recv1, send2, recv2,
):
    a, d = lax.axis_index("ra"), lax.axis_index("dec")
    barrier_signal(na, nd, a, d)
    params[0:5, :] = jnp.exp(flux_ref[...])
    params[5:7, :] = pos_ref[...]
    params[7:8, :] = width_ref[...]
    tile = tile_ref[...]
    rows = tile.shape[1]
    names, rank = ranks_of(tile)
    block = params[...]
    ranked = jnp.concatenate(
        [jnp.where(rank == float(k), block, 0.0) for k in range(RANKS)], axis=0
    )
    gap = jnp.zeros((LANES - ranked.shape[0] * 3, rows), BF16)
    none = jnp.zeros(ranked.shape, BF16)
    pieces = split3(ranked)
    total = None
    for n in range(3):
        hot = jnp.where(names + (n - 1) * nd == tile, 1.0, 0.0).astype(BF16)
        for piece in pieces:
            rhs = jnp.concatenate([piece if m == n else none for m in range(3)] + [gap], axis=0)
            term = dot_tt(hot, rhs)
            total = term if total is None else total + term
    first[...] = total.reshape(na, nd, LANES)
    barrier_wait(na, nd)

    sends = []
    for off in range(1, na):
        peer = lax.rem(a + off, na)
        copy = pltpu.make_async_remote_copy(
            src_ref=first.at[peer], dst_ref=got1.at[a], send_sem=send1.at[off],
            recv_sem=recv1.at[a], device_id=(peer, d), device_id_type=MESH,
        )
        copy.start()
        sends.append(copy)
    got1[a] = first[a]
    stage[0] = jnp.zeros((na, LANES), F32)
    stage[nd + 1] = jnp.zeros((na, LANES), F32)
    for off in range(1, na):
        peer = lax.rem(a + off, na)
        pltpu.make_async_remote_copy(
            src_ref=got1.at[peer], dst_ref=got1.at[peer], send_sem=send1.at[off],
            recv_sem=recv1.at[peer], device_id=(peer, d), device_id_type=MESH,
        ).wait_recv()
    for col in range(nd):
        stage[col + 1] = got1[:, col, :]
    for off in range(1, nd):
        peer = lax.rem(d + off, nd)
        copy = pltpu.make_async_remote_copy(
            src_ref=stage.at[pl.ds(peer, 3)], dst_ref=got2.at[d], send_sem=send2.at[off],
            recv_sem=recv2.at[d], device_id=(a, peer), device_id_type=MESH,
        )
        copy.start()
        sends.append(copy)
    got2[d] = stage[pl.ds(d, 3)]
    for off in range(1, nd):
        peer = lax.rem(d + off, nd)
        pltpu.make_async_remote_copy(
            src_ref=stage.at[pl.ds(peer, 3)], dst_ref=got2.at[peer], send_sem=send2.at[off],
            recv_sem=recv2.at[peer], device_id=(a, peer), device_id_type=MESH,
        ).wait_recv()
    for n in range(3):
        out_ref[n] = got2[:, n].reshape(na * nd, LANES).T
    for copy in sends:
        copy.wait_send()


def return_kernel(
    na, nd, grad_ref, tile_ref, out_ref,
    first, got1, stage, got2, send1, recv1, send2, recv2,
):
    a, d = lax.axis_index("ra"), lax.axis_index("dec")
    barrier_signal(na, nd, a, d)
    for n in range(3):
        first[:, n] = grad_ref[n].T.reshape(nd, na, LANES)
    got1[nd] = jnp.zeros(got1.shape[1:], F32)
    got1[nd + 1] = jnp.zeros(got1.shape[1:], F32)
    got2[na] = jnp.zeros(got2.shape[1:], F32)
    got2[na + 1] = jnp.zeros(got2.shape[1:], F32)
    tile = tile_ref[...]
    names, rank = ranks_of(tile)
    hot = jnp.where(names == tile, 1.0, 0.0).astype(BF16)
    barrier_wait(na, nd)

    sends = []
    for off in range(1, nd):
        peer = lax.rem(d + off, nd)
        copy = pltpu.make_async_remote_copy(
            src_ref=first.at[peer], dst_ref=got1.at[d], send_sem=send1.at[off],
            recv_sem=recv1.at[d], device_id=(a, peer), device_id_type=MESH,
        )
        copy.start()
        sends.append(copy)
    got1[d] = first[d]
    for off in range(1, nd):
        peer = lax.rem(d + off, nd)
        pltpu.make_async_remote_copy(
            src_ref=first.at[peer], dst_ref=got1.at[peer], send_sem=send1.at[off],
            recv_sem=recv1.at[peer], device_id=(a, peer), device_id_type=MESH,
        ).wait_recv()
    for col in range(nd):
        after, before = (col + 1 if col + 1 < nd else nd), (col - 1 if col else nd + 1)
        stage[:, col, :] = got1[after, 0] + got1[col, 1] + got1[before, 2]
    for off in range(1, na):
        peer = lax.rem(a + off, na)
        copy = pltpu.make_async_remote_copy(
            src_ref=stage.at[peer], dst_ref=got2.at[a], send_sem=send2.at[off],
            recv_sem=recv2.at[a], device_id=(peer, d), device_id_type=MESH,
        )
        copy.start()
        sends.append(copy)
    got2[a] = stage[a]
    for off in range(1, na):
        peer = lax.rem(a + off, na)
        pltpu.make_async_remote_copy(
            src_ref=stage.at[peer], dst_ref=got2.at[peer], send_sem=send2.at[off],
            recv_sem=recv2.at[peer], device_id=(peer, d), device_id_type=MESH,
        ).wait_recv()
    mine = got2[0:na].reshape(na * nd, LANES)
    none = jnp.zeros((nd, LANES), F32)
    later = jnp.concatenate([mine[nd:], none], axis=0)
    sooner = jnp.concatenate([none, mine[:-nd]], axis=0)
    held, width = mine.T, 8 * RANKS
    slots = (
        later.T[0:width] + held[width : 2 * width] + sooner.T[2 * width : 3 * width]
    )
    rows = None
    for piece in split3(slots):
        term = dot_nn(piece, hot)
        rows = term if rows is None else rows + term
    total = None
    for k in range(RANKS):
        term = jnp.where(rank == float(k), rows[8 * k : 8 * k + 8], 0.0)
        total = term if total is None else total + term
    out_ref[...] = total
    for copy in sends:
        copy.wait_send()


CORNERS = ((-1, -1), (-1, 1), (1, -1), (1, 1))
SIDES = ((-1, 0), (1, 0), (0, -1), (0, 1))
GROUPS = CORNERS + SIDES + ((0, 0),)
BANDS = 5
STEP = 64
OUTS = BANDS + 6


def compute_kernel(
    side, src_ref, sky_ref, counts_ref, out_ref,
    counts, weights, turned, prof_i, prof_j, low_i, low_j, scaled,
    rim_top, rim_bottom, rim_left, rim_right, sums, count_sem,
):
    slots = RANKS * LANES

    def copy_in(b):
        return pltpu.make_async_copy(counts_ref.at[b], counts.at[b], count_sem.at[b])

    for b in range(BANDS):
        copy_in(b).start()
    index = {group: n for n, group in enumerate(GROUPS)}

    def source(group, k, row):
        dr, dc = group
        start = (dr + 1) * 8 * RANKS + k * 8 + row
        return src_ref[dc + 1, start : start + 1, :]

    def span(step):
        if step == 0:
            return 0, side
        return (0, EDGE) if step < 0 else (side - EDGE, EDGE)

    def make_profile(group, axis, f32_ref, low_ref, scaled_ref):
        first, count = span(group[axis])
        base = first + 0.5 - group[axis] * side
        iota = lax.broadcasted_iota(jnp.int32, (STEP, LANES), 0).astype(F32)
        for k in range(RANKS):
            lanes = slice(k * LANES, (k + 1) * LANES)
            center = source(group, k, 5 + axis)
            inverse = 1.0 / (float(EDGE) * jnp.exp(source(group, k, 7)))
            factor = -HALF_LOG2E * inverse * inverse
            norm = inverse * (1.0 / ROOT_2PI)
            flux = [source(group, k, b) for b in range(BANDS)] if scaled_ref is not None else []

            def body(step, carry):
                start = pl.multiple_of(step * STEP, STEP)
                off = iota + (base + start.astype(F32)) - center
                prof = jnp.exp2(off * factor * off) * norm
                rows = pl.ds(start, STEP)
                f32_ref[rows, lanes] = prof
                if low_ref is not None:
                    low_ref[rows, lanes] = prof.astype(BF16)
                for b, f in enumerate(flux):
                    into = pl.ds(pl.multiple_of(b * count + step * STEP, STEP), STEP)
                    scaled_ref[into, lanes] = (prof * f).astype(BF16)
                return carry

            lax.fori_loop(0, count // STEP, body, 0, unroll=True)

    def rounded(x):
        return x.astype(BF16).astype(F32)

    rims_ij = {-1: rim_top, 1: rim_bottom}
    rims_ji = {-1: rim_left, 1: rim_right}
    for group in SIDES + CORNERS:
        n = index[group]
        dr, dc = group
        if dr:
            make_profile(group, 0, prof_i[n], None, scaled[n])
            make_profile(group, 1, prof_j[n], low_j[n], None)
            part = rounded(dot_tt(scaled[n][...], low_j[n][...]))
            part = part.reshape(BANDS, EDGE, part.shape[1])
            if dc == 0:
                rims_ij[dr][...] = part
            else:
                start = 0 if dc < 0 else side - EDGE
                rims_ij[dr][:, :, start : start + EDGE] += part
        else:
            make_profile(group, 0, prof_i[n], low_i[n], None)
            make_profile(group, 1, prof_j[n], None, scaled[n])
            rims_ji[dc][...] = rounded(dot_tt(low_i[n][...], scaled[n][...]))

    own = index[(0, 0)]
    make_profile((0, 0), 0, prof_i[own], low_i[own], scaled[own])
    make_profile((0, 0), 1, prof_j[own], low_j[own], None)

    for b in range(BANDS):
        model = rounded(dot_tt(scaled[own][b * side : (b + 1) * side, :], low_j[own][...]))
        copy_in(b).wait()
        level = sky_ref[0, 0, b]
        for chunk in range(side // EDGE):
            rows = slice(chunk * EDGE, (chunk + 1) * EDGE)
            for other in range(side // EDGE):
                cols = slice(other * EDGE, (other + 1) * EDGE)
                part = model[rows, cols] + level
                if other == 0:
                    part = part + rim_left[rows, b * EDGE : (b + 1) * EDGE]
                if other == side // EDGE - 1:
                    part = part + rim_right[rows, b * EDGE : (b + 1) * EDGE]
                if chunk == 0:
                    part = part + rim_top[b, :, cols]
                if chunk == side // EDGE - 1:
                    part = part + rim_bottom[b, :, cols]
                ratio = counts[b, rows, cols].astype(F32) / part - 1.0
                low = ratio.astype(BF16)
                weights[b, rows, cols] = low
                turned[cols, b * side + chunk * EDGE : b * side + (chunk + 1) * EDGE] = low.T

    def fold(x):
        return jnp.sum(x.reshape(x.shape[0] // 8, 8, x.shape[1]), axis=0)

    def put(n, k, at, value, add):
        if add:
            sums[n, k, at] += value
        else:
            sums[n, k, at] = value

    def moments(group, axis, k, start, total, prof, base, add):
        n = index[group]
        iota = lax.broadcasted_iota(jnp.int32, (8, LANES), 0).astype(F32)
        zeroth = first = second = None
        for run in range(total.shape[0] // EDGE):
            s0 = s1 = s2 = None
            for row in range(run * EDGE, (run + 1) * EDGE, 8):
                term = prof[row : row + 8] * total[row : row + 8]
                s0 = term if s0 is None else s0 + term
                s1 = s0 if s1 is None else s1 + s0
                s2 = s1 if s2 is None else s2 + s1
            end = iota + (base + (start + (run + 1) * EDGE)) - source(group, k, 5 + axis)
            scaled0 = end * s0
            one = scaled0 - 8.0 * s1
            two = end * (scaled0 - 16.0 * s1) + 64.0 * (s2 + (s2 - s1))
            zeroth = s0 if zeroth is None else zeroth + s0
            first = one if first is None else first + one
            second = two if second is None else second + two
        at = BANDS + 3 * axis
        put(n, k, at, zeroth, add)
        put(n, k, at + 1, first, add)
        put(n, k, at + 2, second, add)

    def per_band(group, axis, lhs, rhs, prof_ref, start, add):
        n = index[group]
        base = span(group[axis])[0] + 0.5 - group[axis] * side
        for pair in range(RANKS // 2):
            wide = slice(pair * 2 * LANES, (pair + 1) * 2 * LANES)
            along = dot_nn(lhs, rhs[:, wide])
            for k in (2 * pair, 2 * pair + 1):
                lanes = slice((k - 2 * pair) * LANES, (k - 2 * pair + 1) * LANES)
                prof = prof_ref[start : start + EDGE, k * LANES : (k + 1) * LANES]
                low = rounded(prof)
                total = None
                for b in range(BANDS):
                    band = along[b * EDGE : (b + 1) * EDGE, lanes]
                    put(n, k, b, fold(low * band), add)
                    term = source(group, k, b) * band
                    total = term if total is None else total + term
                moments(group, axis, k, start, total, prof, base, add)

    def all_bands(group, axis, lhs, scaled_ref, prof_ref):
        base = span(group[axis])[0] + 0.5 - group[axis] * side
        for pair in range(RANKS // 2):
            wide = slice(pair * 2 * LANES, (pair + 1) * 2 * LANES)
            along = dot_nn(lhs, scaled_ref[:, wide])
            for k in (2 * pair, 2 * pair + 1):
                lanes = slice((k - 2 * pair) * LANES, (k - 2 * pair + 1) * LANES)
                prof = prof_ref[:, k * LANES : (k + 1) * LANES]
                moments(group, axis, k, 0, along[:, lanes], prof, base, False)

    for group in SIDES + CORNERS:
        n = index[group]
        (r0, rn), (c0, cn) = span(group[0]), span(group[1])
        if group[0]:
            lhs = weights[:, r0 : r0 + rn, c0 : c0 + cn].reshape(BANDS * rn, cn)
            per_band(group, 0, lhs, low_j[n], prof_i[n], 0, False)
            lhs = jnp.concatenate(
                [turned[c0 : c0 + cn, b * side + r0 : b * side + r0 + rn] for b in range(BANDS)],
                axis=1,
            )
            all_bands(group, 1, lhs, scaled[n], prof_j[n])
        else:
            lhs = jnp.concatenate(
                [turned[c0 : c0 + cn, b * side : (b + 1) * side] for b in range(BANDS)], axis=0
            )
            per_band(group, 1, lhs, low_i[n], prof_j[n], 0, False)
            lhs = jnp.concatenate([weights[b, :, c0 : c0 + cn] for b in range(BANDS)], axis=1)
            all_bands(group, 0, lhs, scaled[n], prof_i[n])

    for start in range(0, side, EDGE):
        lhs = weights[:, start : start + EDGE, :].reshape(BANDS * EDGE, side)
        per_band((0, 0), 0, lhs, low_j[own], prof_i[own], start, start > 0)
    all_bands((0, 0), 1, turned[...], scaled[own], prof_j[own])

    out_ref[...] = jnp.zeros_like(out_ref)
    for group in GROUPS:
        n, (dr, dc) = index[group], group
        for k in range(RANKS):
            inverse = 1.0 / (float(EDGE) * jnp.exp(source(group, k, 7)))
            square = inverse * inverse

            def total(which):
                return jnp.sum(sums[n, k, which], axis=0, keepdims=True)

            start = (dr + 1) * 8 * RANKS + k * 8
            for b in range(BANDS):
                out_ref[dc + 1, start + b : start + b + 1, :] = source(group, k, b) * total(b)
            zeroth = total(BANDS) + total(BANDS + 3)
            second = total(BANDS + 2) + total(BANDS + 5)
            out_ref[dc + 1, start + 5 : start + 6, :] = total(BANDS + 1) * square
            out_ref[dc + 1, start + 6 : start + 7, :] = total(BANDS + 4) * square
            out_ref[dc + 1, start + 7 : start + 8, :] = second * square - zeroth


def compute_call(side, na, nd, routed, sky_level, counts):
    slots = RANKS * LANES
    dma = pltpu.SemaphoreType.DMA

    def extent(step):
        return EDGE if step else side

    prof_i = [pltpu.VMEM((extent(g[0]), slots), F32) for g in GROUPS]
    prof_j = [pltpu.VMEM((extent(g[1]), slots), F32) for g in GROUPS]
    low_i = [pltpu.VMEM((extent(g[0]) if g[0] == 0 else 16, slots), BF16) for g in GROUPS]
    low_j = [pltpu.VMEM((extent(g[1]) if g[0] or not g[1] else 16, slots), BF16) for g in GROUPS]
    scaled = [pltpu.VMEM((BANDS * (EDGE if g != (0, 0) else side), slots), BF16) for g in GROUPS]
    return pl.pallas_call(
        functools.partial(compute_kernel, side),
        out_shape=jax.ShapeDtypeStruct((3, LANES, na * nd), F32),
        in_specs=[
            VMEM,
            pl.BlockSpec(memory_space=pltpu.SMEM),
            pl.BlockSpec(memory_space=pl.ANY),
        ],
        out_specs=VMEM,
        scratch_shapes=[
            pltpu.VMEM((BANDS, side, side), jnp.int32),
            pltpu.VMEM((BANDS, side, side), BF16),
            pltpu.VMEM((side, BANDS * side), BF16),
            prof_i, prof_j, low_i, low_j, scaled,
            pltpu.VMEM((BANDS, EDGE, side), F32),
            pltpu.VMEM((BANDS, EDGE, side), F32),
            pltpu.VMEM((side, BANDS * EDGE), F32),
            pltpu.VMEM((side, BANDS * EDGE), F32),
            pltpu.VMEM((len(GROUPS), RANKS, OUTS, 8, LANES), F32),
            dma((BANDS,)),
        ],
        compiler_params=pltpu.CompilerParams(vmem_limit_bytes=60 << 20),
        name="compute",
    )(routed, sky_level, counts)


def on_device(na, nd, log_flux, position, log_width, owner_tile, sky_level, counts):
    rows = log_flux.shape[1]
    side = counts.shape[1]
    width = log_width.reshape(1, rows)
    tile = owner_tile.reshape(1, rows)
    dma = pltpu.SemaphoreType.DMA

    routed = pl.pallas_call(
        functools.partial(route_kernel, na, nd),
        out_shape=jax.ShapeDtypeStruct((3, LANES, na * nd), F32),
        in_specs=[VMEM] * 4,
        out_specs=VMEM,
        scratch_shapes=[
            pltpu.VMEM((8, rows), F32),
            pltpu.VMEM((na, nd, LANES), F32),
            pltpu.VMEM((na, nd, LANES), F32),
            pltpu.VMEM((nd + 2, na, LANES), F32),
            pltpu.VMEM((nd, 3, na, LANES), F32),
            dma((na,)), dma((na,)), dma((nd,)), dma((nd,)),
        ],
        compiler_params=pltpu.CompilerParams(collective_id=0, has_side_effects=True),
        name="route",
    )(log_flux, position, width, tile)

    partial = compute_call(side, na, nd, routed, sky_level, counts)

    return pl.pallas_call(
        functools.partial(return_kernel, na, nd),
        out_shape=jax.ShapeDtypeStruct((8, rows), F32),
        in_specs=[VMEM] * 2,
        out_specs=VMEM,
        scratch_shapes=[
            pltpu.VMEM((nd, 3, na, LANES), F32),
            pltpu.VMEM((nd + 2, 3, na, LANES), F32),
            pltpu.VMEM((na, nd, LANES), F32),
            pltpu.VMEM((na + 2, nd, LANES), F32),
            dma((nd,)), dma((nd,)), dma((na,)), dma((na,)),
        ],
        compiler_params=pltpu.CompilerParams(collective_id=1, has_side_effects=True),
        name="give_back",
    )(partial, tile)


def solution(mesh):
    na, nd = mesh.shape["ra"], mesh.shape["dec"]
    in_specs = (
        P(None, ("ra", "dec")),
        P(None, ("ra", "dec")),
        P(("ra", "dec")),
        P(("ra", "dec"), None),
        P("ra", "dec", None),
        P(None, "ra", "dec"),
    )
    return jax.shard_map(
        functools.partial(on_device, na, nd),
        mesh=mesh,
        in_specs=in_specs,
        out_specs=P(None, ("ra", "dec")),
        check_vma=False,
    )
```

```python
import functools
import math

import jax
import jax.numpy as jnp
from jax import lax
from jax.experimental import pallas as pl
from jax.experimental.pallas import tpu as pltpu
from jax.sharding import PartitionSpec as P

F32 = jnp.float32
BF16 = jnp.bfloat16
MESH = pl.DeviceIdType.MESH
VMEM = pl.BlockSpec(memory_space=pltpu.VMEM)

EDGE = 128
RANKS = 4
LANES = 128
HALF_LOG2E = 0.5 * math.log2(math.e)
ROOT_2PI = math.sqrt(2.0 * math.pi)


def split3(x):
    hi = x.astype(BF16)
    rest = x - hi.astype(F32)
    mid = rest.astype(BF16)
    lo = (rest - mid.astype(F32)).astype(BF16)
    return hi, mid, lo


def dot_tt(a, b):
    return lax.dot_general(a, b, (((1,), (1,)), ((), ())), preferred_element_type=F32)


def dot_nn(a, b):
    return lax.dot_general(a, b, (((1,), (0,)), ((), ())), preferred_element_type=F32)


def ranks_of(tile):
    rows = tile.shape[1]
    names = lax.broadcasted_iota(jnp.int32, (LANES, rows), 0)
    onehot = names == tile
    earlier = lax.broadcasted_iota(jnp.int32, (rows, rows), 0) < lax.broadcasted_iota(
        jnp.int32, (rows, rows), 1
    )
    before = dot_nn(
        jnp.where(onehot, 1.0, 0.0).astype(BF16), jnp.where(earlier, 1.0, 0.0).astype(BF16)
    )
    rank = jnp.sum(jnp.where(onehot, before, 0.0), axis=0, keepdims=True)
    return names, rank


def barrier_signal(na, nd, a, d):
    barrier = pltpu.get_barrier_semaphore()
    for off in range(1, na):
        pl.semaphore_signal(
            barrier, inc=1, device_id=(lax.rem(a + off, na), d), device_id_type=MESH
        )
    for off in range(1, nd):
        pl.semaphore_signal(
            barrier, inc=1, device_id=(a, lax.rem(d + off, nd)), device_id_type=MESH
        )


def barrier_wait(na, nd):
    pl.semaphore_wait(pltpu.get_barrier_semaphore(), na - 1 + nd - 1)


def route(
    na, nd, flux_ref, pos_ref, width_ref, tile_ref, out_ref,
    params, first, got1, stage, got2, send1, recv1, send2, recv2,
):
    a, d = lax.axis_index("ra"), lax.axis_index("dec")
    barrier_signal(na, nd, a, d)
    params[0:5, :] = jnp.exp(flux_ref[...])
    params[5:7, :] = pos_ref[...]
    params[7:8, :] = width_ref[...]
    tile = tile_ref[...]
    rows = tile.shape[1]
    names, rank = ranks_of(tile)
    block = params[...]
    ranked = jnp.concatenate(
        [jnp.where(rank == float(k), block, 0.0) for k in range(RANKS)], axis=0
    )
    gap = jnp.zeros((LANES - ranked.shape[0] * 3, rows), BF16)
    none = jnp.zeros(ranked.shape, BF16)
    pieces = split3(ranked)
    total = None
    for n in range(3):
        hot = jnp.where(names + (n - 1) * nd == tile, 1.0, 0.0).astype(BF16)
        for piece in pieces:
            rhs = jnp.concatenate([piece if m == n else none for m in range(3)] + [gap], axis=0)
            term = dot_tt(hot, rhs)
            total = term if total is None else total + term
    first[...] = total.reshape(na, nd, LANES)
    barrier_wait(na, nd)

    sends = []
    for off in range(1, na):
        peer = lax.rem(a + off, na)
        copy = pltpu.make_async_remote_copy(
            src_ref=first.at[peer], dst_ref=got1.at[a], send_sem=send1.at[off],
            recv_sem=recv1.at[a], device_id=(peer, d), device_id_type=MESH,
        )
        copy.start()
        sends.append(copy)
    got1[a] = first[a]
    stage[0] = jnp.zeros((na, LANES), F32)
    stage[nd + 1] = jnp.zeros((na, LANES), F32)
    for off in range(1, na):
        peer = lax.rem(a + off, na)
        pltpu.make_async_remote_copy(
            src_ref=got1.at[peer], dst_ref=got1.at[peer], send_sem=send1.at[off],
            recv_sem=recv1.at[peer], device_id=(peer, d), device_id_type=MESH,
        ).wait_recv()
    for col in range(nd):
        stage[col + 1] = got1[:, col, :]
    for off in range(1, nd):
        peer = lax.rem(d + off, nd)
        copy = pltpu.make_async_remote_copy(
            src_ref=stage.at[pl.ds(peer, 3)], dst_ref=got2.at[d], send_sem=send2.at[off],
            recv_sem=recv2.at[d], device_id=(a, peer), device_id_type=MESH,
        )
        copy.start()
        sends.append(copy)
    got2[d] = stage[pl.ds(d, 3)]
    for off in range(1, nd):
        peer = lax.rem(d + off, nd)
        pltpu.make_async_remote_copy(
            src_ref=stage.at[pl.ds(peer, 3)], dst_ref=got2.at[peer], send_sem=send2.at[off],
            recv_sem=recv2.at[peer], device_id=(a, peer), device_id_type=MESH,
        ).wait_recv()
    for n in range(3):
        out_ref[n] = got2[:, n].reshape(na * nd, LANES).T
    return sends


def give_back(
    na, nd, grad_ref, tile_ref, out_ref,
    first, got1, stage, got2, send1, recv1, send2, recv2,
):
    a, d = lax.axis_index("ra"), lax.axis_index("dec")
    for n in range(3):
        first[:, n] = grad_ref[n].T.reshape(nd, na, LANES)

    sends = []
    for off in range(1, nd):
        peer = lax.rem(d + off, nd)
        copy = pltpu.make_async_remote_copy(
            src_ref=first.at[peer], dst_ref=got1.at[d], send_sem=send1.at[off],
            recv_sem=recv1.at[d], device_id=(a, peer), device_id_type=MESH,
        )
        copy.start()
        sends.append(copy)
    got1[d] = first[d]
    for off in range(1, nd):
        peer = lax.rem(d + off, nd)
        pltpu.make_async_remote_copy(
            src_ref=first.at[peer], dst_ref=got1.at[peer], send_sem=send1.at[off],
            recv_sem=recv1.at[peer], device_id=(a, peer), device_id_type=MESH,
        ).wait_recv()
    for col in range(nd):
        part = got1[col, 1]
        if col + 1 < nd:
            part = part + got1[col + 1, 0]
        if col:
            part = part + got1[col - 1, 2]
        stage[:, col, :] = part
    for off in range(1, na):
        peer = lax.rem(a + off, na)
        copy = pltpu.make_async_remote_copy(
            src_ref=stage.at[peer], dst_ref=got2.at[a], send_sem=send2.at[off],
            recv_sem=recv2.at[a], device_id=(peer, d), device_id_type=MESH,
        )
        copy.start()
        sends.append(copy)
    got2[a] = stage[a]
    for off in range(1, na):
        peer = lax.rem(a + off, na)
        pltpu.make_async_remote_copy(
            src_ref=stage.at[peer], dst_ref=got2.at[peer], send_sem=send2.at[off],
            recv_sem=recv2.at[peer], device_id=(peer, d), device_id_type=MESH,
        ).wait_recv()
    tile = tile_ref[...]
    names, rank = ranks_of(tile)
    hot = jnp.where(names == tile, 1.0, 0.0).astype(BF16)
    mine = got2[...].reshape(na * nd, LANES)
    none = jnp.zeros((nd, LANES), F32)
    later = jnp.concatenate([mine[nd:], none], axis=0)
    sooner = jnp.concatenate([none, mine[:-nd]], axis=0)
    held, width = mine.T, 8 * RANKS
    slots = (
        later.T[0:width] + held[width : 2 * width] + sooner.T[2 * width : 3 * width]
    )
    rows = None
    for piece in split3(slots):
        term = dot_nn(piece, hot)
        rows = term if rows is None else rows + term
    for k in range(RANKS):
        part = slice(8 * k, 8 * k + 8)
        out_ref[part, :] = jnp.where(rank == float(k), rows[part], 0.0)
    return sends


CORNERS = ((-1, -1), (-1, 1), (1, -1), (1, 1))
SIDES = ((-1, 0), (1, 0), (0, -1), (0, 1))
GROUPS = CORNERS + SIDES + ((0, 0),)
BANDS = 5
STEP = 64
OUTS = BANDS + 6


def compute(
    side, src_ref, sky_ref, copy_in, out_ref,
    counts, weights, turned, prof_i, prof_j, low_i, low_j, scaled,
    rim_top, rim_bottom, rim_left, rim_right, sums,
):
    index = {group: n for n, group in enumerate(GROUPS)}

    def source(group, k, row):
        dr, dc = group
        start = (dr + 1) * 8 * RANKS + k * 8 + row
        return src_ref[dc + 1, start : start + 1, :]

    def span(step):
        if step == 0:
            return 0, side
        return (0, EDGE) if step < 0 else (side - EDGE, EDGE)

    def make_profile(group, axis, f32_ref, low_ref, scaled_ref):
        first, count = span(group[axis])
        base = first + 0.5 - group[axis] * side
        iota = lax.broadcasted_iota(jnp.int32, (STEP, LANES), 0).astype(F32)
        for k in range(RANKS):
            lanes = slice(k * LANES, (k + 1) * LANES)
            center = source(group, k, 5 + axis)
            inverse = 1.0 / (float(EDGE) * jnp.exp(source(group, k, 7)))
            factor = -HALF_LOG2E * inverse * inverse
            norm = inverse * (1.0 / ROOT_2PI)
            flux = [source(group, k, b) for b in range(BANDS)] if scaled_ref is not None else []

            def body(step, carry):
                start = pl.multiple_of(step * STEP, STEP)
                off = iota + (base + start.astype(F32)) - center
                prof = jnp.exp2(off * factor * off) * norm
                rows = pl.ds(start, STEP)
                f32_ref[rows, lanes] = prof
                if low_ref is not None:
                    low_ref[rows, lanes] = prof.astype(BF16)
                for b, f in enumerate(flux):
                    into = pl.ds(pl.multiple_of(b * count + step * STEP, STEP), STEP)
                    scaled_ref[into, lanes] = (prof * f).astype(BF16)
                return carry

            lax.fori_loop(0, count // STEP, body, 0, unroll=True)

    def rounded(x):
        return x.astype(BF16).astype(F32)

    rims_ij = {-1: rim_top, 1: rim_bottom}
    rims_ji = {-1: rim_left, 1: rim_right}
    for group in SIDES + CORNERS:
        n = index[group]
        dr, dc = group
        if dr:
            make_profile(group, 0, prof_i[n], None, scaled[n])
            make_profile(group, 1, prof_j[n], low_j[n], None)
            part = rounded(dot_tt(scaled[n][...], low_j[n][...]))
            part = part.reshape(BANDS, EDGE, part.shape[1])
            if dc == 0:
                rims_ij[dr][...] = part
            else:
                start = 0 if dc < 0 else side - EDGE
                rims_ij[dr][:, :, start : start + EDGE] += part
        else:
            make_profile(group, 0, prof_i[n], low_i[n], None)
            make_profile(group, 1, prof_j[n], None, scaled[n])
            rims_ji[dc][...] = rounded(dot_tt(low_i[n][...], scaled[n][...]))

    own = index[(0, 0)]
    make_profile((0, 0), 0, prof_i[own], low_i[own], scaled[own])
    make_profile((0, 0), 1, prof_j[own], low_j[own], None)

    for b in range(BANDS):
        model = rounded(dot_tt(scaled[own][b * side : (b + 1) * side, :], low_j[own][...]))
        copy_in(b).wait()
        level = sky_ref[0, 0, b]
        for chunk in range(side // EDGE):
            rows = slice(chunk * EDGE, (chunk + 1) * EDGE)
            for other in range(side // EDGE):
                cols = slice(other * EDGE, (other + 1) * EDGE)
                part = model[rows, cols] + level
                if other == 0:
                    part = part + rim_left[rows, b * EDGE : (b + 1) * EDGE]
                if other == side // EDGE - 1:
                    part = part + rim_right[rows, b * EDGE : (b + 1) * EDGE]
                if chunk == 0:
                    part = part + rim_top[b, :, cols]
                if chunk == side // EDGE - 1:
                    part = part + rim_bottom[b, :, cols]
                ratio = counts[b, rows, cols].astype(F32) / part - 1.0
                low = ratio.astype(BF16)
                weights[b, rows, cols] = low
                turned[cols, b * side + chunk * EDGE : b * side + (chunk + 1) * EDGE] = low.T

    def fold(x):
        return jnp.sum(x.reshape(x.shape[0] // 8, 8, x.shape[1]), axis=0)

    def put(n, k, at, value, add):
        if add:
            sums[n, k, at] += value
        else:
            sums[n, k, at] = value

    def moments(group, axis, k, start, total, prof, base, add):
        n = index[group]
        iota = lax.broadcasted_iota(jnp.int32, (8, LANES), 0).astype(F32)
        zeroth = first = second = None
        for run in range(total.shape[0] // EDGE):
            s0 = s1 = s2 = None
            for row in range(run * EDGE, (run + 1) * EDGE, 8):
                term = prof[row : row + 8] * total[row : row + 8]
                s0 = term if s0 is None else s0 + term
                s1 = s0 if s1 is None else s1 + s0
                s2 = s1 if s2 is None else s2 + s1
            end = iota + (base + (start + (run + 1) * EDGE)) - source(group, k, 5 + axis)
            scaled0 = end * s0
            one = scaled0 - 8.0 * s1
            two = end * (scaled0 - 16.0 * s1) + 64.0 * (s2 + (s2 - s1))
            zeroth = s0 if zeroth is None else zeroth + s0
            first = one if first is None else first + one
            second = two if second is None else second + two
        at = BANDS + 3 * axis
        put(n, k, at, zeroth, add)
        put(n, k, at + 1, first, add)
        put(n, k, at + 2, second, add)

    def per_band(group, axis, lhs, rhs, prof_ref, start, add):
        n = index[group]
        base = span(group[axis])[0] + 0.5 - group[axis] * side
        for pair in range(RANKS // 2):
            wide = slice(pair * 2 * LANES, (pair + 1) * 2 * LANES)
            along = dot_nn(lhs, rhs[:, wide])
            for k in (2 * pair, 2 * pair + 1):
                lanes = slice((k - 2 * pair) * LANES, (k - 2 * pair + 1) * LANES)
                prof = prof_ref[start : start + EDGE, k * LANES : (k + 1) * LANES]
                low = rounded(prof)
                total = None
                for b in range(BANDS):
                    band = along[b * EDGE : (b + 1) * EDGE, lanes]
                    put(n, k, b, fold(low * band), add)
                    term = source(group, k, b) * band
                    total = term if total is None else total + term
                moments(group, axis, k, start, total, prof, base, add)

    def all_bands(group, axis, lhs, scaled_ref, prof_ref):
        base = span(group[axis])[0] + 0.5 - group[axis] * side
        for pair in range(RANKS // 2):
            wide = slice(pair * 2 * LANES, (pair + 1) * 2 * LANES)
            along = dot_nn(lhs, scaled_ref[:, wide])
            for k in (2 * pair, 2 * pair + 1):
                lanes = slice((k - 2 * pair) * LANES, (k - 2 * pair + 1) * LANES)
                prof = prof_ref[:, k * LANES : (k + 1) * LANES]
                moments(group, axis, k, 0, along[:, lanes], prof, base, False)

    for group in SIDES + CORNERS:
        n = index[group]
        (r0, rn), (c0, cn) = span(group[0]), span(group[1])
        if group[0]:
            lhs = weights[:, r0 : r0 + rn, c0 : c0 + cn].reshape(BANDS * rn, cn)
            per_band(group, 0, lhs, low_j[n], prof_i[n], 0, False)
            lhs = jnp.concatenate(
                [turned[c0 : c0 + cn, b * side + r0 : b * side + r0 + rn] for b in range(BANDS)],
                axis=1,
            )
            all_bands(group, 1, lhs, scaled[n], prof_j[n])
        else:
            lhs = jnp.concatenate(
                [turned[c0 : c0 + cn, b * side : (b + 1) * side] for b in range(BANDS)], axis=0
            )
            per_band(group, 1, lhs, low_i[n], prof_j[n], 0, False)
            lhs = jnp.concatenate([weights[b, :, c0 : c0 + cn] for b in range(BANDS)], axis=1)
            all_bands(group, 0, lhs, scaled[n], prof_i[n])

    for start in range(0, side, EDGE):
        lhs = weights[:, start : start + EDGE, :].reshape(BANDS * EDGE, side)
        per_band((0, 0), 0, lhs, low_j[own], prof_i[own], start, start > 0)
    all_bands((0, 0), 1, turned[...], scaled[own], prof_j[own])

    out_ref[...] = jnp.zeros_like(out_ref)
    for group in GROUPS:
        n, (dr, dc) = index[group], group
        for k in range(RANKS):
            inverse = 1.0 / (float(EDGE) * jnp.exp(source(group, k, 7)))
            square = inverse * inverse

            def total(which):
                return jnp.sum(sums[n, k, which], axis=0, keepdims=True)

            start = (dr + 1) * 8 * RANKS + k * 8
            for b in range(BANDS):
                out_ref[dc + 1, start + b : start + b + 1, :] = source(group, k, b) * total(b)
            zeroth = total(BANDS) + total(BANDS + 3)
            second = total(BANDS + 2) + total(BANDS + 5)
            out_ref[dc + 1, start + 5 : start + 6, :] = total(BANDS + 1) * square
            out_ref[dc + 1, start + 6 : start + 7, :] = total(BANDS + 4) * square
            out_ref[dc + 1, start + 7 : start + 8, :] = second * square - zeroth


def fused_kernel(
    na, nd, side, flux_ref, pos_ref, width_ref, tile_ref, sky_ref, counts_ref, out_ref,
    counts, count_sem, sources, partial, to_route, to_compute, to_return,
):
    def copy_in(b):
        return pltpu.make_async_copy(counts_ref.at[b], counts.at[b], count_sem.at[b])

    for b in range(BANDS):
        copy_in(b).start()
    sends = route(na, nd, flux_ref, pos_ref, width_ref, tile_ref, sources, *to_route)
    compute(side, sources, sky_ref, copy_in, partial, counts, *to_compute)
    sends += give_back(na, nd, partial, tile_ref, out_ref, *to_return)
    for copy in sends:
        copy.wait_send()


def on_device(na, nd, log_flux, position, log_width, owner_tile, sky_level, counts):
    rows = log_flux.shape[1]
    side = counts.shape[1]
    slots = RANKS * LANES
    width = log_width.reshape(1, rows)
    tile = owner_tile.reshape(1, rows)
    dma = pltpu.SemaphoreType.DMA

    def extent(step):
        return EDGE if step else side

    def buffer(*shape, dtype=F32):
        return pltpu.VMEM(shape, dtype)

    spare = 16
    masked = pl.pallas_call(
        functools.partial(fused_kernel, na, nd, side),
        out_shape=jax.ShapeDtypeStruct((RANKS * 8, rows), F32),
        in_specs=[VMEM] * 4
        + [pl.BlockSpec(memory_space=pltpu.SMEM), pl.BlockSpec(memory_space=pl.ANY)],
        out_specs=VMEM,
        scratch_shapes=[
            buffer(BANDS, side, side, dtype=jnp.int32),
            dma((BANDS,)),
            buffer(3, LANES, na * nd),
            buffer(3, LANES, na * nd),
            [
                buffer(8, rows),
                buffer(na, nd, LANES),
                buffer(na, nd, LANES),
                buffer(nd + 2, na, LANES),
                buffer(nd, 3, na, LANES),
                dma((na,)), dma((na,)), dma((nd,)), dma((nd,)),
            ],
            [
                buffer(BANDS, side, side, dtype=BF16),
                buffer(side, BANDS * side, dtype=BF16),
                [buffer(extent(g[0]), slots) for g in GROUPS],
                [buffer(extent(g[1]), slots) for g in GROUPS],
                [buffer(spare if g[0] else side, slots, dtype=BF16) for g in GROUPS],
                [
                    buffer(extent(g[1]) if g[0] or not g[1] else spare, slots, dtype=BF16)
                    for g in GROUPS
                ],
                [buffer(BANDS * (EDGE if any(g) else side), slots, dtype=BF16) for g in GROUPS],
                buffer(BANDS, EDGE, side),
                buffer(BANDS, EDGE, side),
                buffer(side, BANDS * EDGE),
                buffer(side, BANDS * EDGE),
                buffer(len(GROUPS), RANKS, OUTS, 8, LANES),
            ],
            [
                buffer(nd, 3, na, LANES),
                buffer(nd, 3, na, LANES),
                buffer(na, nd, LANES),
                buffer(na, nd, LANES),
                dma((nd,)), dma((nd,)), dma((na,)), dma((na,)),
            ],
        ],
        compiler_params=pltpu.CompilerParams(
            collective_id=0, has_side_effects=True, vmem_limit_bytes=60 << 20
        ),
        name="fused",
    )(log_flux, position, width, tile, sky_level, counts)
    return jnp.sum(masked.reshape(RANKS, 8, rows), axis=0)


def solution(mesh):
    na, nd = mesh.shape["ra"], mesh.shape["dec"]
    in_specs = (
        P(None, ("ra", "dec")),
        P(None, ("ra", "dec")),
        P(("ra", "dec")),
        P(("ra", "dec"), None),
        P("ra", "dec", None),
        P(None, "ra", "dec"),
    )
    return jax.shard_map(
        functools.partial(on_device, na, nd),
        mesh=mesh,
        in_specs=in_specs,
        out_specs=P(None, ("ra", "dec")),
        check_vma=False,
    )
```

```python
import functools
import math

import jax
import jax.numpy as jnp
from jax import lax
from jax.experimental import pallas as pl
from jax.experimental.pallas import tpu as pltpu
from jax.sharding import PartitionSpec as P

F32 = jnp.float32
BF16 = jnp.bfloat16
MESH = pl.DeviceIdType.MESH
VMEM = pl.BlockSpec(memory_space=pltpu.VMEM)

EDGE = 128
RANKS = 4
LANES = 128
HALF_LOG2E = 0.5 * math.log2(math.e)
ROOT_2PI = math.sqrt(2.0 * math.pi)


def split3(x):
    hi = x.astype(BF16)
    rest = x - hi.astype(F32)
    mid = rest.astype(BF16)
    lo = (rest - mid.astype(F32)).astype(BF16)
    return hi, mid, lo


def dot_tt(a, b):
    return lax.dot_general(a, b, (((1,), (1,)), ((), ())), preferred_element_type=F32)


def dot_nn(a, b):
    return lax.dot_general(a, b, (((1,), (0,)), ((), ())), preferred_element_type=F32)


def ranks_of(tile):
    rows = tile.shape[1]
    names = lax.broadcasted_iota(jnp.int32, (LANES, rows), 0)
    onehot = names == tile
    earlier = lax.broadcasted_iota(jnp.int32, (rows, rows), 0) < lax.broadcasted_iota(
        jnp.int32, (rows, rows), 1
    )
    before = dot_nn(
        jnp.where(onehot, 1.0, 0.0).astype(BF16), jnp.where(earlier, 1.0, 0.0).astype(BF16)
    )
    rank = jnp.sum(jnp.where(onehot, before, 0.0), axis=0, keepdims=True)
    return names, rank


def far_first(na, nd):
    ring_x, ring_z = na // 4, nd // 2
    along_ra = [(x, y, core) for x in range(ring_x) for y in range(2) for core in range(2)][1:]
    along_ra.sort(key=lambda o: -(4 * min(o[0], ring_x - o[0]) + 8 * o[1] + o[2]))
    along_dec = [(z, y) for z in range(ring_z) for y in range(2)][1:]
    along_dec.sort(key=lambda o: -(2 * min(o[0], ring_z - o[0]) + 2 * o[1]))
    a, d = lax.axis_index("ra"), lax.axis_index("dec")
    ra = [
        lax.rem(a // 4 + x, ring_x) * 4 + lax.rem(a // 2 + y, 2) * 2 + lax.rem(a + core, 2)
        for x, y, core in along_ra
    ]
    dec = [lax.rem(d // 2 + z, ring_z) * 2 + lax.rem(d + y, 2) for z, y in along_dec]
    return a, d, ra, dec


def send(src, dst, send_sem, recv_sem, a, d):
    return pltpu.make_async_remote_copy(
        src_ref=src, dst_ref=dst, send_sem=send_sem, recv_sem=recv_sem,
        device_id=(a, d), device_id_type=MESH,
    )


def greet(peers):
    a, d, ra, dec = peers
    barrier = pltpu.get_barrier_semaphore()
    for peer in ra:
        pl.semaphore_signal(barrier, inc=1, device_id=(peer, d), device_id_type=MESH)
    for peer in dec:
        pl.semaphore_signal(barrier, inc=1, device_id=(a, peer), device_id_type=MESH)


def route(
    na, nd, peers, fetched, out_ref,
    flux, position, width, tiles, params, onehot, ranks, first, got1, stage, got2,
    send1, recv1, send2, recv2,
):
    a, d, ra, dec = peers
    stage[0] = jnp.zeros((na, LANES), F32)
    stage[nd + 1] = jnp.zeros((na, LANES), F32)
    for copy in fetched:
        copy.wait()
    params[0:5, :] = jnp.exp(flux[...])
    params[5:7, :] = position[...]
    params[7:8, :] = width[...]
    tile = tiles[...]
    rows = tile.shape[1]
    names, rank = ranks_of(tile)
    ranks[...] = rank
    onehot[...] = jnp.where(names == tile, 1.0, 0.0).astype(BF16)
    block = params[...]
    ranked = jnp.concatenate(
        [jnp.where(rank == float(k), block, 0.0) for k in range(RANKS)], axis=0
    )
    gap = jnp.zeros((LANES - ranked.shape[0] * 3, rows), BF16)
    none = jnp.zeros(ranked.shape, BF16)
    pieces = split3(ranked)
    total = None
    for n in range(3):
        hot = jnp.where(names + (n - 1) * nd == tile, 1.0, 0.0).astype(BF16)
        for piece in pieces:
            rhs = jnp.concatenate([piece if m == n else none for m in range(3)] + [gap], axis=0)
            term = dot_tt(hot, rhs)
            total = term if total is None else total + term
    first[...] = total.reshape(na, nd, LANES)
    pl.semaphore_wait(pltpu.get_barrier_semaphore(), len(ra) + len(dec))

    sends = []
    for i, peer in enumerate(ra):
        copy = send(first.at[peer], got1.at[a], send1.at[i], recv1.at[a], peer, d)
        copy.start()
        sends.append(copy)
    got1[a] = first[a]
    for i, peer in enumerate(ra):
        send(first.at[peer], got1.at[peer], send1.at[i], recv1.at[peer], peer, d).wait_recv()
    for col in range(nd):
        stage[col + 1] = got1[:, col, :]
    for i, peer in enumerate(dec):
        copy = send(
            stage.at[pl.ds(peer, 3)], got2.at[d], send2.at[i], recv2.at[d], a, peer
        )
        copy.start()
        sends.append(copy)
    got2[d] = stage[pl.ds(d, 3)]
    for i, peer in enumerate(dec):
        send(
            stage.at[pl.ds(peer, 3)], got2.at[peer], send2.at[i], recv2.at[peer], a, peer
        ).wait_recv()
    for n in range(3):
        out_ref[n] = got2[:, n].reshape(na * nd, LANES).T
    return sends


class GiveBack:
    def __init__(self, na, nd, peers, grad_ref, first, got1, stage, got2, send1, recv1, send2, recv2):
        self.na, self.nd, self.peers, self.grad_ref = na, nd, peers, grad_ref
        self.first, self.got1, self.stage, self.got2 = first, got1, stage, got2
        self.send1, self.recv1, self.send2, self.recv2 = send1, recv1, send2, recv2
        self.sends = []

    def along_dec(self, n, i, place):
        a, _, _, dec = self.peers
        return send(
            self.first.at[n, dec[i]], self.got1.at[n, place],
            self.send1.at[n, i], self.recv1.at[n, place], a, dec[i],
        )

    def start(self, n):
        _, d, _, dec = self.peers
        self.first[n] = self.grad_ref[n].T.reshape(self.nd, self.na, LANES)
        for i in range(len(dec)):
            copy = self.along_dec(n, i, d)
            copy.start()
            self.sends.append(copy)
        self.got1[n, d] = self.first[n, d]

    def finish(self, onehot, ranks, out_ref):
        na, nd, got1, stage, got2 = self.na, self.nd, self.got1, self.stage, self.got2
        a, d, ra, dec = self.peers
        for n in (0, 2, 1):
            for i, peer in enumerate(dec):
                self.along_dec(n, i, peer).wait_recv()
        for col in range(nd):
            part = got1[1, col]
            if col + 1 < nd:
                part = part + got1[0, col + 1]
            if col:
                part = part + got1[2, col - 1]
            stage[:, col, :] = part
        for i, peer in enumerate(ra):
            copy = send(stage.at[peer], got2.at[a], self.send2.at[i], self.recv2.at[a], peer, d)
            copy.start()
            self.sends.append(copy)
        got2[a] = stage[a]
        for i, peer in enumerate(ra):
            send(
                stage.at[peer], got2.at[peer], self.send2.at[i], self.recv2.at[peer], peer, d
            ).wait_recv()
        mine = got2[...].reshape(na * nd, LANES)
        none = jnp.zeros((nd, LANES), F32)
        later = jnp.concatenate([mine[nd:], none], axis=0)
        sooner = jnp.concatenate([none, mine[:-nd]], axis=0)
        held, width = mine.T, 8 * RANKS
        slots = (
            later.T[0:width] + held[width : 2 * width] + sooner.T[2 * width : 3 * width]
        )
        rows = None
        for piece in split3(slots):
            term = dot_nn(piece, onehot[...])
            rows = term if rows is None else rows + term
        rank = ranks[...]
        for k in range(RANKS):
            part = slice(8 * k, 8 * k + 8)
            out_ref[part, :] = jnp.where(rank == float(k), rows[part], 0.0)
        for copy in self.sends:
            copy.wait_send()


CORNERS = ((-1, -1), (-1, 1), (1, -1), (1, 1))
SIDES = ((-1, 0), (1, 0), (0, -1), (0, 1))
GROUPS = CORNERS + SIDES + ((0, 0),)
BANDS = 5
STEP = 64
OUTS = BANDS + 6


def compute(
    side, src_ref, sky_ref, copy_in, out_ref, done,
    counts, weights, turned, prof_i, prof_j, low_i, low_j, scaled,
    rim_top, rim_bottom, rim_left, rim_right, sums,
):
    index = {group: n for n, group in enumerate(GROUPS)}

    def source(group, k, row):
        dr, dc = group
        start = (dr + 1) * 8 * RANKS + k * 8 + row
        return src_ref[dc + 1, start : start + 1, :]

    def span(step):
        if step == 0:
            return 0, side
        return (0, EDGE) if step < 0 else (side - EDGE, EDGE)

    def make_profile(group, axis, f32_ref, low_ref, scaled_ref):
        first, count = span(group[axis])
        base = first + 0.5 - group[axis] * side
        iota = lax.broadcasted_iota(jnp.int32, (STEP, LANES), 0).astype(F32)
        for k in range(RANKS):
            lanes = slice(k * LANES, (k + 1) * LANES)
            center = source(group, k, 5 + axis)
            inverse = 1.0 / (float(EDGE) * jnp.exp(source(group, k, 7)))
            factor = -HALF_LOG2E * inverse * inverse
            norm = inverse * (1.0 / ROOT_2PI)
            flux = [source(group, k, b) for b in range(BANDS)] if scaled_ref is not None else []

            def body(step, carry):
                start = pl.multiple_of(step * STEP, STEP)
                off = iota + (base + start.astype(F32)) - center
                prof = jnp.exp2(off * factor * off) * norm
                rows = pl.ds(start, STEP)
                f32_ref[rows, lanes] = prof
                if low_ref is not None:
                    low_ref[rows, lanes] = prof.astype(BF16)
                for b, f in enumerate(flux):
                    into = pl.ds(pl.multiple_of(b * count + step * STEP, STEP), STEP)
                    scaled_ref[into, lanes] = (prof * f).astype(BF16)
                return carry

            lax.fori_loop(0, count // STEP, body, 0, unroll=True)

    def rounded(x):
        return x.astype(BF16).astype(F32)

    class Pipeline:
        def __init__(self):
            self.held = None

        def add(self, product, consume):
            value = product()
            self.flush()
            self.held = functools.partial(consume, value)

        def flush(self):
            if self.held is not None:
                self.held()
            self.held = None

    line = Pipeline()
    rims_ij = {-1: rim_top, 1: rim_bottom}
    rims_ji = {-1: rim_left, 1: rim_right}
    own = index[(0, 0)]

    def profiles(group):
        n = index[group]
        by_row = group[0] or not group[1]
        make_profile(group, 0, prof_i[n], None if group[0] else low_i[n], scaled[n] if by_row else None)
        make_profile(group, 1, prof_j[n], low_j[n] if by_row else None, None if by_row else scaled[n])

    def render(group):
        n = index[group]
        if group[0] or not group[1]:
            return dot_tt(scaled[n][...], low_j[n][...])
        return dot_tt(low_i[n][...], scaled[n][...])

    def add_rim(group, model):
        dr, dc = group
        if dr:
            part = rounded(model).reshape(BANDS, EDGE, model.shape[1])
            if dc == 0:
                rims_ij[dr][...] = part
            else:
                start = 0 if dc < 0 else side - EDGE
                rims_ij[dr][:, :, start : start + EDGE] += part
        else:
            rims_ji[dc][...] = rounded(model)

    around = SIDES + CORNERS
    profiles(around[0])
    for here, following in zip(around, around[1:] + ((0, 0),)):
        profiles(following)
        line.add(functools.partial(render, here), functools.partial(add_rim, here))

    def own_model(b):
        return dot_tt(scaled[own][b * side : (b + 1) * side, :], low_j[own][...])

    def weigh(b, model):
        level = sky_ref[0, 0:1, b : b + 1]
        for chunk in range(side // EDGE):
            rows = slice(chunk * EDGE, (chunk + 1) * EDGE)
            for other in range(side // EDGE):
                cols = slice(other * EDGE, (other + 1) * EDGE)
                part = rounded(model[rows, cols]) + level
                if other == 0:
                    part = part + rim_left[rows, b * EDGE : (b + 1) * EDGE]
                if other == side // EDGE - 1:
                    part = part + rim_right[rows, b * EDGE : (b + 1) * EDGE]
                if chunk == 0:
                    part = part + rim_top[b, :, cols]
                if chunk == side // EDGE - 1:
                    part = part + rim_bottom[b, :, cols]
                ratio = counts[b, rows, cols].astype(F32) / part - 1.0
                low = ratio.astype(BF16)
                weights[b, rows, cols] = low
                turned[cols, b * side + chunk * EDGE : b * side + (chunk + 1) * EDGE] = low.T

    for b in range(BANDS):
        copy_in(b).wait()
    for b in range(BANDS):
        line.add(functools.partial(own_model, b), functools.partial(weigh, b))
    line.flush()

    def fold(x):
        return jnp.sum(x.reshape(x.shape[0] // 8, 8, x.shape[1]), axis=0)

    def put(n, k, at, value, add):
        if add:
            sums[n, k, at] += value
        else:
            sums[n, k, at] = value

    def moments(group, axis, k, start, total, prof, base, add):
        n = index[group]
        iota = lax.broadcasted_iota(jnp.int32, (8, LANES), 0).astype(F32)
        zeroth = first = second = None
        for run in range(total.shape[0] // EDGE):
            s0 = s1 = s2 = None
            for row in range(run * EDGE, (run + 1) * EDGE, 8):
                term = prof[row : row + 8] * total[row : row + 8]
                s0 = term if s0 is None else s0 + term
                s1 = s0 if s1 is None else s1 + s0
                s2 = s1 if s2 is None else s2 + s1
            end = iota + (base + (start + (run + 1) * EDGE)) - source(group, k, 5 + axis)
            scaled0 = end * s0
            one = scaled0 - 8.0 * s1
            two = end * (scaled0 - 16.0 * s1) + 64.0 * (s2 + (s2 - s1))
            zeroth = s0 if zeroth is None else zeroth + s0
            first = one if first is None else first + one
            second = two if second is None else second + two
        at = BANDS + 3 * axis
        put(n, k, at, zeroth, add)
        put(n, k, at + 1, first, add)
        put(n, k, at + 2, second, add)

    def per_band(group, axis, lhs, rhs, prof_ref, start, add):
        n = index[group]
        base = span(group[axis])[0] + 0.5 - group[axis] * side

        def consume(pair, along):
            for k in (2 * pair, 2 * pair + 1):
                lanes = slice((k - 2 * pair) * LANES, (k - 2 * pair + 1) * LANES)
                prof = prof_ref[start : start + EDGE, k * LANES : (k + 1) * LANES]
                low = rounded(prof)
                total = None
                for b in range(BANDS):
                    band = along[b * EDGE : (b + 1) * EDGE, lanes]
                    put(n, k, b, fold(low * band), add)
                    term = source(group, k, b) * band
                    total = term if total is None else total + term
                moments(group, axis, k, start, total, prof, base, add)

        for pair in range(RANKS // 2):
            wide = slice(pair * 2 * LANES, (pair + 1) * 2 * LANES)
            line.add(
                lambda wide=wide: dot_nn(lhs(), rhs[:, wide]), functools.partial(consume, pair)
            )

    def all_bands(group, axis, lhs, scaled_ref, prof_ref):
        base = span(group[axis])[0] + 0.5 - group[axis] * side

        def consume(pair, along):
            for k in (2 * pair, 2 * pair + 1):
                lanes = slice((k - 2 * pair) * LANES, (k - 2 * pair + 1) * LANES)
                prof = prof_ref[:, k * LANES : (k + 1) * LANES]
                moments(group, axis, k, 0, along[:, lanes], prof, base, False)

        for pair in range(RANKS // 2):
            wide = slice(pair * 2 * LANES, (pair + 1) * 2 * LANES)
            line.add(
                lambda wide=wide: dot_nn(lhs(), scaled_ref[:, wide]),
                functools.partial(consume, pair),
            )

    def near_rows(group):
        (r0, rn), (c0, cn) = span(group[0]), span(group[1])
        return weights[:, r0 : r0 + rn, c0 : c0 + cn].reshape(BANDS * rn, cn)

    def far_cols(group):
        (r0, rn), (c0, cn) = span(group[0]), span(group[1])
        at = [b * side + r0 for b in range(BANDS)]
        return jnp.concatenate([turned[c0 : c0 + cn, r : r + rn] for r in at], axis=1)

    def near_cols(group):
        c0, cn = span(group[1])
        at = [b * side for b in range(BANDS)]
        return jnp.concatenate([turned[c0 : c0 + cn, r : r + side] for r in at], axis=0)

    def far_rows(group):
        c0, cn = span(group[1])
        return jnp.concatenate([weights[b, :, c0 : c0 + cn] for b in range(BANDS)], axis=1)

    def side_grads(group):
        n = index[group]
        if group[0]:
            lhs = functools.partial(near_rows, group)
            per_band(group, 0, lhs, low_j[n], prof_i[n], 0, False)
            all_bands(group, 1, functools.partial(far_cols, group), scaled[n], prof_j[n])
        else:
            lhs = functools.partial(near_cols, group)
            per_band(group, 1, lhs, low_i[n], prof_j[n], 0, False)
            all_bands(group, 0, functools.partial(far_rows, group), scaled[n], prof_i[n])

    def own_rows(start):
        return weights[:, start : start + EDGE, :].reshape(BANDS * EDGE, side)

    def own_grads():
        for start in range(0, side, EDGE):
            lhs = functools.partial(own_rows, start)
            per_band((0, 0), 0, lhs, low_j[own], prof_i[own], start, start > 0)
        all_bands((0, 0), 1, lambda: turned[...], scaled[own], prof_j[own])

    def collect(group):
        n, (dr, dc) = index[group], group
        for k in range(RANKS):
            inverse = 1.0 / (float(EDGE) * jnp.exp(source(group, k, 7)))
            square = inverse * inverse

            def total(which):
                return jnp.sum(sums[n, k, which], axis=0, keepdims=True)

            start = (dr + 1) * 8 * RANKS + k * 8
            for b in range(BANDS):
                out_ref[dc + 1, start + b : start + b + 1, :] = source(group, k, b) * total(b)
            zeroth = total(BANDS) + total(BANDS + 3)
            second = total(BANDS + 2) + total(BANDS + 5)
            out_ref[dc + 1, start + 5 : start + 6, :] = total(BANDS + 1) * square
            out_ref[dc + 1, start + 6 : start + 7, :] = total(BANDS + 4) * square
            out_ref[dc + 1, start + 7 : start + 8, :] = second * square - zeroth

    for step in (-1, 1, 0):
        groups = [group for group in around if group[1] == step]
        for group in groups:
            side_grads(group)
        if step == 0:
            own_grads()
            groups.append((0, 0))
        line.flush()
        out_ref[step + 1] = jnp.zeros(out_ref.shape[1:], F32)
        for group in groups:
            collect(group)
        done(step + 1)


def fused_kernel(
    na, nd, side, flux_ref, pos_ref, width_ref, tile_ref, sky_ref, counts_ref, out_ref,
    counts, count_sem, sky, flux, position, width, tiles, input_sem, onehot, ranks,
    sources, partial, to_route, to_compute, to_return,
):
    peers = far_first(na, nd)
    greet(peers)
    fetched = [
        pltpu.make_async_copy(src, dst, input_sem.at[n])
        for n, (src, dst) in enumerate(
            [
                (tile_ref, tiles), (flux_ref, flux), (pos_ref, position),
                (width_ref, width), (sky_ref, sky),
            ]
        )
    ]
    for copy in fetched:
        copy.start()

    def copy_in(b):
        return pltpu.make_async_copy(counts_ref.at[b], counts.at[b], count_sem.at[b])

    for b in range(BANDS):
        copy_in(b).start()
    params, *rest = to_route
    sends = route(
        na, nd, peers, fetched, sources, flux, position, width, tiles, params, onehot, ranks, *rest
    )
    back = GiveBack(na, nd, peers, partial, *to_return)
    compute(side, sources, sky, copy_in, partial, back.start, counts, *to_compute)
    back.finish(onehot, ranks, out_ref)
    for copy in sends:
        copy.wait_send()


def buffer(*shape, dtype=F32):
    return pltpu.VMEM(shape, dtype)


def compute_buffers(side):
    slots = RANKS * LANES
    spare = 16

    def extent(step):
        return EDGE if step else side

    return [
        buffer(BANDS, side, side, dtype=BF16),
        buffer(side, BANDS * side, dtype=BF16),
        [buffer(extent(g[0]), slots) for g in GROUPS],
        [buffer(extent(g[1]), slots) for g in GROUPS],
        [buffer(spare if g[0] else side, slots, dtype=BF16) for g in GROUPS],
        [
            buffer(extent(g[1]) if g[0] or not g[1] else spare, slots, dtype=BF16)
            for g in GROUPS
        ],
        [buffer(BANDS * (EDGE if any(g) else side), slots, dtype=BF16) for g in GROUPS],
        buffer(BANDS, EDGE, side),
        buffer(BANDS, EDGE, side),
        buffer(side, BANDS * EDGE),
        buffer(side, BANDS * EDGE),
        buffer(len(GROUPS), RANKS, OUTS, 8, LANES),
    ]


def on_device(na, nd, log_flux, position, log_width, owner_tile, sky_level, counts):
    rows = log_flux.shape[1]
    side = counts.shape[1]
    width = log_width.reshape(1, rows)
    tile = owner_tile.reshape(1, rows)
    dma = pltpu.SemaphoreType.DMA

    masked = pl.pallas_call(
        functools.partial(fused_kernel, na, nd, side),
        out_shape=jax.ShapeDtypeStruct((RANKS * 8, rows), F32),
        in_specs=[pl.BlockSpec(memory_space=pl.ANY)] * 6,
        out_specs=VMEM,
        scratch_shapes=[
            buffer(BANDS, side, side, dtype=jnp.int32),
            dma((BANDS,)),
            buffer(*sky_level.shape),
            buffer(*log_flux.shape),
            buffer(*position.shape),
            buffer(1, rows),
            buffer(1, rows, dtype=jnp.int32),
            dma((5,)),
            buffer(LANES, rows, dtype=BF16),
            buffer(1, rows),
            buffer(3, LANES, na * nd),
            buffer(3, LANES, na * nd),
            [
                buffer(8, rows),
                buffer(na, nd, LANES),
                buffer(na, nd, LANES),
                buffer(nd + 2, na, LANES),
                buffer(nd, 3, na, LANES),
                dma((na,)), dma((na,)), dma((nd,)), dma((nd,)),
            ],
            compute_buffers(side),
            [
                buffer(3, nd, na, LANES),
                buffer(3, nd, na, LANES),
                buffer(na, nd, LANES),
                buffer(na, nd, LANES),
                dma((3, nd)), dma((3, nd)), dma((na,)), dma((na,)),
            ],
        ],
        compiler_params=pltpu.CompilerParams(
            collective_id=0, has_side_effects=True, vmem_limit_bytes=60 << 20
        ),
        name="fused",
    )(log_flux, position, width, tile, sky_level, counts)
    return jnp.sum(masked.reshape(RANKS, 8, rows), axis=0)


def solution(mesh):
    na, nd = mesh.shape["ra"], mesh.shape["dec"]
    in_specs = (
        P(None, ("ra", "dec")),
        P(None, ("ra", "dec")),
        P(("ra", "dec")),
        P(("ra", "dec"), None),
        P("ra", "dec", None),
        P(None, "ra", "dec"),
    )
    return jax.shard_map(
        functools.partial(on_device, na, nd),
        mesh=mesh,
        in_specs=in_specs,
        out_specs=P(None, ("ra", "dec")),
        check_vma=False,
    )
```

```python
import functools
import math

import jax
import jax.numpy as jnp
from jax import lax
from jax.experimental import pallas as pl
from jax.experimental.pallas import tpu as pltpu
from jax.sharding import PartitionSpec as P

F32 = jnp.float32
BF16 = jnp.bfloat16
MESH = pl.DeviceIdType.MESH
VMEM = pl.BlockSpec(memory_space=pltpu.VMEM)

EDGE = 128
RANKS = 4
LANES = 128
HALF_LOG2E = 0.5 * math.log2(math.e)
ROOT_2PI = math.sqrt(2.0 * math.pi)


def split3(x):
    hi = x.astype(BF16)
    rest = x - hi.astype(F32)
    mid = rest.astype(BF16)
    lo = (rest - mid.astype(F32)).astype(BF16)
    return hi, mid, lo


def dot_tt(a, b):
    return lax.dot_general(a, b, (((1,), (1,)), ((), ())), preferred_element_type=F32)


def dot_nn(a, b):
    return lax.dot_general(a, b, (((1,), (0,)), ((), ())), preferred_element_type=F32)


def ranks_of(tile):
    rows = tile.shape[1]
    names = lax.broadcasted_iota(jnp.int32, (LANES, rows), 0)
    onehot = names == tile
    earlier = lax.broadcasted_iota(jnp.int32, (rows, rows), 0) < lax.broadcasted_iota(
        jnp.int32, (rows, rows), 1
    )
    before = dot_nn(
        jnp.where(onehot, 1.0, 0.0).astype(BF16), jnp.where(earlier, 1.0, 0.0).astype(BF16)
    )
    rank = jnp.sum(jnp.where(onehot, before, 0.0), axis=0, keepdims=True)
    return names, rank


class Place:
    def __init__(self, na, nd):
        ring_x, ring_z = na // 4, nd // 2
        a, d = lax.axis_index("ra"), lax.axis_index("dec")
        x, h, k, z, low = a // 4, lax.rem(a // 2, 2), lax.rem(a, 2), d // 2, lax.rem(d, 2)
        self.far_count, self.near_count, self.ring_z = ring_x * ring_z, 8, ring_z
        self.low, self.far_here, self.near_here = low, x * ring_z + z, h * 4 + k * 2 + low
        steps = [(i, j) for i in range(ring_x) for j in range(ring_z)][1:]
        steps.sort(key=lambda o: -(min(o[0], ring_x - o[0]) + min(o[1], ring_z - o[1])))
        self.far = []
        for i, j in steps:
            px, pz = lax.rem(x + i, ring_x), lax.rem(z + j, ring_z)
            self.far.append((px * 4 + h * 2 + k, pz * 2 + low, px * ring_z + pz))
        turns = [(i, j, m) for i in range(2) for j in range(2) for m in range(2)][1:]
        turns.sort(key=lambda o: -(4 * o[0] - 2 * o[0] * o[2] + 2 * o[2] + o[1]))
        self.near = []
        for i, j, m in turns:
            ph, pk, pl_ = lax.rem(h + i, 2), lax.rem(k + j, 2), lax.rem(low + m, 2)
            self.near.append((x * 4 + ph * 2 + pk, z * 2 + pl_, ph * 4 + pk * 2 + pl_))


REACH = 6
SIDE_REACH = 4


def reached(na, nd, ring_z, column, rows):
    number = lax.broadcasted_iota(jnp.int32, (LANES, rows), 0)
    bits = ring_z.bit_length() - 1
    step = number & 7
    a = lax.shift_right_logical(number, 3 + bits) * 4 - 1 + step
    d = (lax.shift_right_logical(number, 3) & (ring_z - 1)) * 2 - 1 + column
    known = (step < REACH) & (a >= 0) & (a < na) & (d >= 0) & (d < nd)
    return jnp.where(known, a * nd + d, -1)


def send(src, dst, send_sem, recv_sem, a, d):
    return pltpu.make_async_remote_copy(
        src_ref=src, dst_ref=dst, send_sem=send_sem, recv_sem=recv_sem,
        device_id=(a, d), device_id_type=MESH,
    )


def greet(place):
    barrier = pltpu.get_barrier_semaphore()
    for a, d, _ in place.far + place.near:
        pl.semaphore_signal(barrier, inc=1, device_id=(a, d), device_id_type=MESH)


def route(
    na, nd, place, fetched, out_ref,
    flux, position, width, tiles, params, onehot, ranks, first, got1, stage, got2,
    send1, recv1, send2, recv2,
):
    for copy in fetched:
        copy.wait()
    params[0:5, :] = jnp.exp(flux[...])
    params[5:7, :] = position[...]
    params[7:8, :] = width[...]
    tile = tiles[...]
    rows = tile.shape[1]
    _, rank = ranks_of(tile)
    ranks[...] = rank
    block = params[...]
    ranked = jnp.concatenate(
        [jnp.where(rank == float(k), block, 0.0) for k in range(RANKS)], axis=0
    )
    none = jnp.zeros(ranked.shape, BF16)
    pieces = split3(ranked)
    total = None
    for n in range(SIDE_REACH):
        names = reached(na, nd, place.ring_z, n, rows)
        hot = jnp.where(names == tile, 1.0, 0.0).astype(BF16)
        onehot[n] = hot
        for piece in pieces:
            rhs = jnp.concatenate([piece if m == n else none for m in range(SIDE_REACH)], axis=0)
            term = dot_tt(hot, rhs)
            total = term if total is None else total + term
    first[...] = total.reshape(first.shape)
    pl.semaphore_wait(pltpu.get_barrier_semaphore(), len(place.far) + len(place.near))

    sends = []
    here = place.far_here
    for i, (a, d, peer) in enumerate(place.far):
        copy = send(first.at[peer], got1.at[here], send1.at[i], recv1.at[here], a, d)
        copy.start()
        sends.append(copy)
    got1[here] = first[here]
    for i, (a, d, peer) in enumerate(place.far):
        send(first.at[peer], got1.at[peer], send1.at[i], recv1.at[peer], a, d).wait_recv()
    for step in range(REACH):
        stage[step] = got1[:, step, :]
    here = place.near_here
    for i, (a, d, peer) in enumerate(place.near):
        part = stage.at[pl.ds(peer // 2, 3)]
        copy = send(part, got2.at[here], send2.at[i], recv2.at[here], a, d)
        copy.start()
        sends.append(copy)
    got2[here] = stage[pl.ds(here // 2, 3)]
    for i, (a, d, peer) in enumerate(place.near):
        part = stage.at[pl.ds(peer // 2, 3)]
        send(part, got2.at[peer], send2.at[i], recv2.at[peer], a, d).wait_recv()
    for n in range(3):
        turned = got2[:, n].reshape(LANES, LANES).T
        out_ref[n] = jnp.where(place.low == 1, pltpu.roll(turned, LANES - 8 * RANKS, 0), turned)
    return sends


class GiveBack:
    def __init__(self, place, grad_ref, first, got1, stage, got2, send1, recv1, send2, recv2):
        self.place, self.grad_ref = place, grad_ref
        self.first, self.got1, self.stage, self.got2 = first, got1, stage, got2
        self.send1, self.recv1, self.send2, self.recv2 = send1, recv1, send2, recv2
        self.sends = []
        stage[...] = jnp.zeros_like(stage)

    def to_near(self, n, i, number):
        a, d, peer = self.place.near[i]
        return send(
            self.first.at[n, peer], self.got1.at[n, number],
            self.send1.at[n, i], self.recv1.at[n, number], a, d,
        )

    def start(self, n):
        place, grads = self.place, self.grad_ref[n]
        grads = jnp.where(place.low == 1, pltpu.roll(grads, 8 * RANKS, 0), grads)
        self.first[n] = grads.T.reshape(self.first.shape[1:])
        for i in range(len(place.near)):
            copy = self.to_near(n, i, place.near_here)
            copy.start()
            self.sends.append(copy)
        self.got1[n, place.near_here] = self.first[n, place.near_here]

    def finish(self, onehot, ranks, out_ref):
        place, got1, stage, got2 = self.place, self.got1, self.stage, self.got2
        for n in (0, 2, 1):
            for i, (_, _, peer) in enumerate(place.near):
                self.to_near(n, i, peer).wait_recv()
        for step in range(REACH):
            part = None
            for n in range(3):
                for number in range(place.near_count):
                    if number // 2 + n == step:
                        part = got1[n, number] if part is None else part + got1[n, number]
            stage[:, step, :] = part
        here = place.far_here
        for i, (a, d, peer) in enumerate(place.far):
            copy = send(
                stage.at[peer], got2.at[here], self.send2.at[i], self.recv2.at[here], a, d
            )
            copy.start()
            self.sends.append(copy)
        got2[here] = stage[here]
        for i, (a, d, peer) in enumerate(place.far):
            send(
                stage.at[peer], got2.at[peer], self.send2.at[i], self.recv2.at[peer], a, d
            ).wait_recv()
        held, width = got2[...].reshape(LANES, LANES).T, 8 * RANKS
        rows = None
        for n in range(SIDE_REACH):
            for piece in split3(held[n * width : (n + 1) * width]):
                term = dot_nn(piece, onehot[n])
                rows = term if rows is None else rows + term
        rank = ranks[...]
        for k in range(RANKS):
            part = slice(8 * k, 8 * k + 8)
            out_ref[part, :] = jnp.where(rank == float(k), rows[part], 0.0)
        for copy in self.sends:
            copy.wait_send()


CORNERS = ((-1, -1), (-1, 1), (1, -1), (1, 1))
SIDES = ((-1, 0), (1, 0), (0, -1), (0, 1))
GROUPS = CORNERS + SIDES + ((0, 0),)
BANDS = 5
STEP = 64
OUTS = BANDS + 6


def compute(
    side, src_ref, sky_ref, copy_in, out_ref, done,
    counts, weights, turned, prof_i, prof_j, low_i, low_j, scaled,
    rim_top, rim_bottom, rim_left, rim_right, sums,
):
    index = {group: n for n, group in enumerate(GROUPS)}

    def source(group, k, row):
        dr, dc = group
        start = (dc + 1) * 8 * RANKS + k * 8 + row
        return src_ref[dr + 1, start : start + 1, :]

    def span(step):
        if step == 0:
            return 0, side
        return (0, EDGE) if step < 0 else (side - EDGE, EDGE)

    def make_profile(group, axis, f32_ref, low_ref, scaled_ref):
        first, count = span(group[axis])
        base = first + 0.5 - group[axis] * side
        iota = lax.broadcasted_iota(jnp.int32, (STEP, LANES), 0).astype(F32)
        for k in range(RANKS):
            lanes = slice(k * LANES, (k + 1) * LANES)
            center = source(group, k, 5 + axis)
            inverse = 1.0 / (float(EDGE) * jnp.exp(source(group, k, 7)))
            factor = -HALF_LOG2E * inverse * inverse
            norm = inverse * (1.0 / ROOT_2PI)
            flux = [source(group, k, b) for b in range(BANDS)] if scaled_ref is not None else []

            def body(step, carry):
                start = pl.multiple_of(step * STEP, STEP)
                off = iota + (base + start.astype(F32)) - center
                prof = jnp.exp2(off * factor * off) * norm
                rows = pl.ds(start, STEP)
                f32_ref[rows, lanes] = prof
                if low_ref is not None:
                    low_ref[rows, lanes] = prof.astype(BF16)
                for b, f in enumerate(flux):
                    into = pl.ds(pl.multiple_of(b * count + step * STEP, STEP), STEP)
                    scaled_ref[into, lanes] = (prof * f).astype(BF16)
                return carry

            lax.fori_loop(0, count // STEP, body, 0, unroll=True)

    def rounded(x):
        return x.astype(BF16).astype(F32)

    class Pipeline:
        def __init__(self):
            self.held = None

        def add(self, product, consume):
            value = product()
            self.flush()
            self.held = functools.partial(consume, value)

        def flush(self):
            if self.held is not None:
                self.held()
            self.held = None

    line = Pipeline()
    rims_ij = {-1: rim_top, 1: rim_bottom}
    rims_ji = {-1: rim_left, 1: rim_right}
    own = index[(0, 0)]

    def profiles(group):
        n = index[group]
        by_row = group[0] or not group[1]
        make_profile(group, 0, prof_i[n], None if group[0] else low_i[n], scaled[n] if by_row else None)
        make_profile(group, 1, prof_j[n], low_j[n] if by_row else None, None if by_row else scaled[n])

    def render(group):
        n = index[group]
        if group[0] or not group[1]:
            return dot_tt(scaled[n][...], low_j[n][...])
        return dot_tt(low_i[n][...], scaled[n][...])

    def add_rim(group, model):
        dr, dc = group
        if dr:
            part = rounded(model).reshape(BANDS, EDGE, model.shape[1])
            if dc == 0:
                rims_ij[dr][...] = part
            else:
                start = 0 if dc < 0 else side - EDGE
                rims_ij[dr][:, :, start : start + EDGE] += part
        else:
            rims_ji[dc][...] = rounded(model)

    around = SIDES + CORNERS
    profiles(around[0])
    for here, following in zip(around, around[1:] + ((0, 0),)):
        profiles(following)
        line.add(functools.partial(render, here), functools.partial(add_rim, here))

    def own_model(b):
        return dot_tt(scaled[own][b * side : (b + 1) * side, :], low_j[own][...])

    def weigh(b, model):
        level = sky_ref[0, 0:1, b : b + 1]
        for chunk in range(side // EDGE):
            rows = slice(chunk * EDGE, (chunk + 1) * EDGE)
            for other in range(side // EDGE):
                cols = slice(other * EDGE, (other + 1) * EDGE)
                part = rounded(model[rows, cols]) + level
                if other == 0:
                    part = part + rim_left[rows, b * EDGE : (b + 1) * EDGE]
                if other == side // EDGE - 1:
                    part = part + rim_right[rows, b * EDGE : (b + 1) * EDGE]
                if chunk == 0:
                    part = part + rim_top[b, :, cols]
                if chunk == side // EDGE - 1:
                    part = part + rim_bottom[b, :, cols]
                ratio = counts[b, rows, cols].astype(F32) / part - 1.0
                low = ratio.astype(BF16)
                weights[b, rows, cols] = low
                turned[cols, b * side + chunk * EDGE : b * side + (chunk + 1) * EDGE] = low.T

    for b in range(BANDS):
        copy_in(b).wait()
    for b in range(BANDS):
        line.add(functools.partial(own_model, b), functools.partial(weigh, b))
    line.flush()

    def fold(x):
        return jnp.sum(x.reshape(x.shape[0] // 8, 8, x.shape[1]), axis=0)

    def put(n, k, at, value, add):
        if add:
            sums[n, k, at] += value
        else:
            sums[n, k, at] = value

    def moments(group, axis, k, start, total, prof, base, add):
        n = index[group]
        iota = lax.broadcasted_iota(jnp.int32, (8, LANES), 0).astype(F32)
        zeroth = first = second = None
        for run in range(total.shape[0] // EDGE):
            s0 = s1 = s2 = None
            for row in range(run * EDGE, (run + 1) * EDGE, 8):
                term = prof[row : row + 8] * total[row : row + 8]
                s0 = term if s0 is None else s0 + term
                s1 = s0 if s1 is None else s1 + s0
                s2 = s1 if s2 is None else s2 + s1
            end = iota + (base + (start + (run + 1) * EDGE)) - source(group, k, 5 + axis)
            scaled0 = end * s0
            one = scaled0 - 8.0 * s1
            two = end * (scaled0 - 16.0 * s1) + 64.0 * (s2 + (s2 - s1))
            zeroth = s0 if zeroth is None else zeroth + s0
            first = one if first is None else first + one
            second = two if second is None else second + two
        at = BANDS + 3 * axis
        put(n, k, at, zeroth, add)
        put(n, k, at + 1, first, add)
        put(n, k, at + 2, second, add)

    def per_band(group, axis, lhs, rhs, prof_ref, start, add):
        n = index[group]
        base = span(group[axis])[0] + 0.5 - group[axis] * side

        def consume(pair, along):
            for k in (2 * pair, 2 * pair + 1):
                lanes = slice((k - 2 * pair) * LANES, (k - 2 * pair + 1) * LANES)
                prof = prof_ref[start : start + EDGE, k * LANES : (k + 1) * LANES]
                low = rounded(prof)
                total = None
                for b in range(BANDS):
                    band = along[b * EDGE : (b + 1) * EDGE, lanes]
                    put(n, k, b, fold(low * band), add)
                    term = source(group, k, b) * band
                    total = term if total is None else total + term
                moments(group, axis, k, start, total, prof, base, add)

        for pair in range(RANKS // 2):
            wide = slice(pair * 2 * LANES, (pair + 1) * 2 * LANES)
            line.add(
                lambda wide=wide: dot_nn(lhs(), rhs[:, wide]), functools.partial(consume, pair)
            )

    def all_bands(group, axis, lhs, scaled_ref, prof_ref):
        base = span(group[axis])[0] + 0.5 - group[axis] * side

        def consume(pair, along):
            for k in (2 * pair, 2 * pair + 1):
                lanes = slice((k - 2 * pair) * LANES, (k - 2 * pair + 1) * LANES)
                prof = prof_ref[:, k * LANES : (k + 1) * LANES]
                moments(group, axis, k, 0, along[:, lanes], prof, base, False)

        for pair in range(RANKS // 2):
            wide = slice(pair * 2 * LANES, (pair + 1) * 2 * LANES)
            line.add(
                lambda wide=wide: dot_nn(lhs(), scaled_ref[:, wide]),
                functools.partial(consume, pair),
            )

    def near_rows(group):
        (r0, rn), (c0, cn) = span(group[0]), span(group[1])
        return weights[:, r0 : r0 + rn, c0 : c0 + cn].reshape(BANDS * rn, cn)

    def far_cols(group):
        (r0, rn), (c0, cn) = span(group[0]), span(group[1])
        at = [b * side + r0 for b in range(BANDS)]
        return jnp.concatenate([turned[c0 : c0 + cn, r : r + rn] for r in at], axis=1)

    def near_cols(group):
        c0, cn = span(group[1])
        at = [b * side for b in range(BANDS)]
        return jnp.concatenate([turned[c0 : c0 + cn, r : r + side] for r in at], axis=0)

    def far_rows(group):
        c0, cn = span(group[1])
        return jnp.concatenate([weights[b, :, c0 : c0 + cn] for b in range(BANDS)], axis=1)

    def side_grads(group):
        n = index[group]
        if group[0]:
            lhs = functools.partial(near_rows, group)
            per_band(group, 0, lhs, low_j[n], prof_i[n], 0, False)
            all_bands(group, 1, functools.partial(far_cols, group), scaled[n], prof_j[n])
        else:
            lhs = functools.partial(near_cols, group)
            per_band(group, 1, lhs, low_i[n], prof_j[n], 0, False)
            all_bands(group, 0, functools.partial(far_rows, group), scaled[n], prof_i[n])

    def own_rows(start):
        return weights[:, start : start + EDGE, :].reshape(BANDS * EDGE, side)

    def own_grads():
        for start in range(0, side, EDGE):
            lhs = functools.partial(own_rows, start)
            per_band((0, 0), 0, lhs, low_j[own], prof_i[own], start, start > 0)
        all_bands((0, 0), 1, lambda: turned[...], scaled[own], prof_j[own])

    def collect(group):
        n, (dr, dc) = index[group], group
        for k in range(RANKS):
            inverse = 1.0 / (float(EDGE) * jnp.exp(source(group, k, 7)))
            square = inverse * inverse

            def total(which):
                return jnp.sum(sums[n, k, which], axis=0, keepdims=True)

            start = (dc + 1) * 8 * RANKS + k * 8
            for b in range(BANDS):
                out_ref[dr + 1, start + b : start + b + 1, :] = source(group, k, b) * total(b)
            zeroth = total(BANDS) + total(BANDS + 3)
            second = total(BANDS + 2) + total(BANDS + 5)
            out_ref[dr + 1, start + 5 : start + 6, :] = total(BANDS + 1) * square
            out_ref[dr + 1, start + 6 : start + 7, :] = total(BANDS + 4) * square
            out_ref[dr + 1, start + 7 : start + 8, :] = second * square - zeroth

    for step in (-1, 1, 0):
        groups = [group for group in around if group[0] == step]
        for group in groups:
            side_grads(group)
        if step == 0:
            own_grads()
            groups.append((0, 0))
        line.flush()
        out_ref[step + 1] = jnp.zeros(out_ref.shape[1:], F32)
        for group in groups:
            collect(group)
        done(step + 1)


def fused_kernel(
    na, nd, side, flux_ref, pos_ref, width_ref, tile_ref, sky_ref, counts_ref, out_ref,
    counts, count_sem, sky, flux, position, width, tiles, input_sem, onehot, ranks,
    sources, partial, to_route, to_compute, to_return,
):
    place = Place(na, nd)
    greet(place)
    fetched = [
        pltpu.make_async_copy(src, dst, input_sem.at[n])
        for n, (src, dst) in enumerate(
            [
                (tile_ref, tiles), (flux_ref, flux), (pos_ref, position),
                (width_ref, width), (sky_ref, sky),
            ]
        )
    ]
    for copy in fetched:
        copy.start()

    def copy_in(b):
        return pltpu.make_async_copy(counts_ref.at[b], counts.at[b], count_sem.at[b])

    for b in range(BANDS):
        copy_in(b).start()
    params, *rest = to_route
    sends = route(
        na, nd, place, fetched, sources, flux, position, width, tiles, params, onehot, ranks, *rest
    )
    back = GiveBack(place, partial, *to_return)
    compute(side, sources, sky, copy_in, partial, back.start, counts, *to_compute)
    back.finish(onehot, ranks, out_ref)
    for copy in sends:
        copy.wait_send()


def buffer(*shape, dtype=F32):
    return pltpu.VMEM(shape, dtype)


def compute_buffers(side):
    slots = RANKS * LANES
    spare = 16

    def extent(step):
        return EDGE if step else side

    return [
        buffer(BANDS, side, side, dtype=BF16),
        buffer(side, BANDS * side, dtype=BF16),
        [buffer(extent(g[0]), slots) for g in GROUPS],
        [buffer(extent(g[1]), slots) for g in GROUPS],
        [buffer(spare if g[0] else side, slots, dtype=BF16) for g in GROUPS],
        [
            buffer(extent(g[1]) if g[0] or not g[1] else spare, slots, dtype=BF16)
            for g in GROUPS
        ],
        [buffer(BANDS * (EDGE if any(g) else side), slots, dtype=BF16) for g in GROUPS],
        buffer(BANDS, EDGE, side),
        buffer(BANDS, EDGE, side),
        buffer(side, BANDS * EDGE),
        buffer(side, BANDS * EDGE),
        buffer(len(GROUPS), RANKS, OUTS, 8, LANES),
    ]


def on_device(na, nd, log_flux, position, log_width, owner_tile, sky_level, counts):
    rows = log_flux.shape[1]
    side = counts.shape[1]
    width = log_width.reshape(1, rows)
    tile = owner_tile.reshape(1, rows)
    dma = pltpu.SemaphoreType.DMA
    near = 8
    far = na * nd // near

    masked = pl.pallas_call(
        functools.partial(fused_kernel, na, nd, side),
        out_shape=jax.ShapeDtypeStruct((RANKS * 8, rows), F32),
        in_specs=[pl.BlockSpec(memory_space=pl.ANY)] * 6,
        out_specs=VMEM,
        scratch_shapes=[
            buffer(BANDS, side, side, dtype=jnp.int32),
            dma((BANDS,)),
            buffer(*sky_level.shape),
            buffer(*log_flux.shape),
            buffer(*position.shape),
            buffer(1, rows),
            buffer(1, rows, dtype=jnp.int32),
            dma((5,)),
            buffer(SIDE_REACH, LANES, rows, dtype=BF16),
            buffer(1, rows),
            buffer(3, LANES, na * nd),
            buffer(3, LANES, na * nd),
            [
                buffer(8, rows),
                buffer(far, 8, LANES),
                buffer(far, 8, LANES),
                buffer(REACH, far, LANES),
                buffer(near, 3, far, LANES),
                dma((far,)), dma((far,)), dma((near,)), dma((near,)),
            ],
            compute_buffers(side),
            [
                buffer(3, near, far, LANES),
                buffer(3, near, far, LANES),
                buffer(far, 8, LANES),
                buffer(far, 8, LANES),
                dma((3, near)), dma((3, near)), dma((far,)), dma((far,)),
            ],
        ],
        compiler_params=pltpu.CompilerParams(
            collective_id=0, has_side_effects=True, vmem_limit_bytes=60 << 20
        ),
        name="fused",
    )(log_flux, position, width, tile, sky_level, counts)
    return jnp.sum(masked.reshape(RANKS, 8, rows), axis=0)


def solution(mesh):
    na, nd = mesh.shape["ra"], mesh.shape["dec"]
    in_specs = (
        P(None, ("ra", "dec")),
        P(None, ("ra", "dec")),
        P(("ra", "dec")),
        P(("ra", "dec"), None),
        P("ra", "dec", None),
        P(None, "ra", "dec"),
    )
    return jax.shard_map(
        functools.partial(on_device, na, nd),
        mesh=mesh,
        in_specs=in_specs,
        out_specs=P(None, ("ra", "dec")),
        check_vma=False,
    )
```

```python
import functools
import math

import jax
import jax.numpy as jnp
from jax import lax
from jax.experimental import pallas as pl
from jax.experimental.pallas import tpu as pltpu
from jax.sharding import PartitionSpec as P

F32 = jnp.float32
BF16 = jnp.bfloat16
MESH = pl.DeviceIdType.MESH
VMEM = pl.BlockSpec(memory_space=pltpu.VMEM)

EDGE = 128
RANKS = 4
LANES = 128
HALF_LOG2E = 0.5 * math.log2(math.e)
ROOT_2PI = math.sqrt(2.0 * math.pi)


def split3(x):
    hi = x.astype(BF16)
    rest = x - hi.astype(F32)
    mid = rest.astype(BF16)
    lo = (rest - mid.astype(F32)).astype(BF16)
    return hi, mid, lo


def dot_tt(a, b):
    return lax.dot_general(a, b, (((1,), (1,)), ((), ())), preferred_element_type=F32)


def dot_nn(a, b):
    return lax.dot_general(a, b, (((1,), (0,)), ((), ())), preferred_element_type=F32)


def ranks_of(tile):
    rows = tile.shape[1]
    names = lax.broadcasted_iota(jnp.int32, (LANES, rows), 0)
    onehot = names == tile
    earlier = lax.broadcasted_iota(jnp.int32, (rows, rows), 0) < lax.broadcasted_iota(
        jnp.int32, (rows, rows), 1
    )
    before = dot_nn(
        jnp.where(onehot, 1.0, 0.0).astype(BF16), jnp.where(earlier, 1.0, 0.0).astype(BF16)
    )
    rank = jnp.sum(jnp.where(onehot, before, 0.0), axis=0, keepdims=True)
    return names, rank


class Place:
    def __init__(self, na, nd):
        ring_x, ring_z = na // 4, nd // 2
        a, d = lax.axis_index("ra"), lax.axis_index("dec")
        x, h, k, z, low = a // 4, lax.rem(a // 2, 2), lax.rem(a, 2), d // 2, lax.rem(d, 2)
        self.far_count, self.near_count, self.ring_z = ring_x * ring_z, 8, ring_z
        self.low, self.far_here, self.near_here = low, x * ring_z + z, h * 4 + k * 2 + low
        steps = [(i, j) for i in range(ring_x) for j in range(ring_z)][1:]
        steps.sort(key=lambda o: -(min(o[0], ring_x - o[0]) + min(o[1], ring_z - o[1])))
        self.far = []
        for i, j in steps:
            px, pz = lax.rem(x + i, ring_x), lax.rem(z + j, ring_z)
            self.far.append((px * 4 + h * 2 + k, pz * 2 + low, px * ring_z + pz))
        turns = [(i, j, m) for i in range(2) for j in range(2) for m in range(2)][1:]
        turns.sort(key=lambda o: -(4 * o[0] - 2 * o[0] * o[2] + 2 * o[2] + o[1]))
        self.near = []
        for i, j, m in turns:
            ph, pk, pl_ = lax.rem(h + i, 2), lax.rem(k + j, 2), lax.rem(low + m, 2)
            self.near.append((x * 4 + ph * 2 + pk, z * 2 + pl_, ph * 4 + pk * 2 + pl_))


REACH = 6
SIDE_REACH = 4


def reached(na, nd, ring_z, column, rows):
    number = lax.broadcasted_iota(jnp.int32, (LANES, rows), 0)
    bits = ring_z.bit_length() - 1
    step = number & 7
    a = lax.shift_right_logical(number, 3 + bits) * 4 - 1 + step
    d = (lax.shift_right_logical(number, 3) & (ring_z - 1)) * 2 - 1 + column
    known = (step < REACH) & (a >= 0) & (a < na) & (d >= 0) & (d < nd)
    return jnp.where(known, a * nd + d, -1)


def send(src, dst, send_sem, recv_sem, a, d):
    return pltpu.make_async_remote_copy(
        src_ref=src, dst_ref=dst, send_sem=send_sem, recv_sem=recv_sem,
        device_id=(a, d), device_id_type=MESH,
    )


def greet(place):
    barrier = pltpu.get_barrier_semaphore()
    for a, d, _ in place.far + place.near:
        pl.semaphore_signal(barrier, inc=1, device_id=(a, d), device_id_type=MESH)


def route(
    na, nd, place, fetched, out_ref,
    flux, position, width, tiles, params, onehot, ranks, first, got1, stage, got2,
    send1, recv1, send2, recv2,
):
    for copy in fetched:
        copy.wait()
    params[0:5, :] = jnp.exp(flux[...])
    params[5:7, :] = position[...]
    params[7:8, :] = width[...]
    tile = tiles[...]
    rows = tile.shape[1]
    _, rank = ranks_of(tile)
    ranks[...] = rank
    block = params[...]
    ranked = jnp.concatenate(
        [jnp.where(rank == float(k), block, 0.0) for k in range(RANKS)], axis=0
    )
    none = jnp.zeros(ranked.shape, BF16)
    pieces = split3(ranked)
    total = None
    for n in range(SIDE_REACH):
        names = reached(na, nd, place.ring_z, n, rows)
        hot = jnp.where(names == tile, 1.0, 0.0).astype(BF16)
        onehot[n] = hot
        for piece in pieces:
            rhs = jnp.concatenate([piece if m == n else none for m in range(SIDE_REACH)], axis=0)
            term = dot_tt(hot, rhs)
            total = term if total is None else total + term
    first[...] = total.reshape(first.shape)
    pl.semaphore_wait(pltpu.get_barrier_semaphore(), len(place.far) + len(place.near))

    sends = []
    here = place.far_here
    for i, (a, d, peer) in enumerate(place.far):
        copy = send(first.at[peer], got1.at[here], send1.at[i], recv1.at[here], a, d)
        copy.start()
        sends.append(copy)
    got1[here] = first[here]
    for i, (a, d, peer) in enumerate(place.far):
        send(first.at[peer], got1.at[peer], send1.at[i], recv1.at[peer], a, d).wait_recv()
    for step in range(REACH):
        stage[step] = got1[:, step, :]
    here = place.near_here
    for i, (a, d, peer) in enumerate(place.near):
        part = stage.at[pl.ds(peer // 2, 3)]
        copy = send(part, got2.at[here], send2.at[i], recv2.at[here], a, d)
        copy.start()
        sends.append(copy)
    got2[here] = stage[pl.ds(here // 2, 3)]
    for i, (a, d, peer) in enumerate(place.near):
        part = stage.at[pl.ds(peer // 2, 3)]
        send(part, got2.at[peer], send2.at[i], recv2.at[peer], a, d).wait_recv()
    for n in range(3):
        turned = got2[:, n].reshape(LANES, LANES).T
        out_ref[n] = jnp.where(place.low == 1, pltpu.roll(turned, LANES - 8 * RANKS, 0), turned)
    return sends


class GiveBack:
    def __init__(self, place, grad_ref, first, got1, stage, got2, send1, recv1, send2, recv2):
        self.place, self.grad_ref = place, grad_ref
        self.first, self.got1, self.stage, self.got2 = first, got1, stage, got2
        self.send1, self.recv1, self.send2, self.recv2 = send1, recv1, send2, recv2
        self.sends = []
        stage[...] = jnp.zeros_like(stage)

    def to_near(self, i, number):
        a, d, peer = self.place.near[i]
        return send(
            self.first.at[peer], self.got1.at[number], self.send1.at[i], self.recv1.at[number], a, d
        )

    def finish(self, onehot, ranks, out_ref):
        place, got1, stage, got2 = self.place, self.got1, self.stage, self.got2
        for n in range(3):
            grads = self.grad_ref[n]
            grads = jnp.where(place.low == 1, pltpu.roll(grads, 8 * RANKS, 0), grads)
            self.first[:, n] = grads.T.reshape(place.near_count, place.far_count, LANES)
        for i in range(len(place.near)):
            copy = self.to_near(i, place.near_here)
            copy.start()
            self.sends.append(copy)
        got1[place.near_here] = self.first[place.near_here]
        for i, (_, _, peer) in enumerate(place.near):
            self.to_near(i, peer).wait_recv()
        for step in range(REACH):
            part = None
            for n in range(3):
                for number in range(place.near_count):
                    if number // 2 + n == step:
                        part = got1[number, n] if part is None else part + got1[number, n]
            stage[:, step, :] = part
        here = place.far_here
        for i, (a, d, peer) in enumerate(place.far):
            copy = send(
                stage.at[peer], got2.at[here], self.send2.at[i], self.recv2.at[here], a, d
            )
            copy.start()
            self.sends.append(copy)
        got2[here] = stage[here]
        for i, (a, d, peer) in enumerate(place.far):
            send(
                stage.at[peer], got2.at[peer], self.send2.at[i], self.recv2.at[peer], a, d
            ).wait_recv()
        held, width = got2[...].reshape(LANES, LANES).T, 8 * RANKS
        rows = None
        for n in range(SIDE_REACH):
            for piece in split3(held[n * width : (n + 1) * width]):
                term = dot_nn(piece, onehot[n])
                rows = term if rows is None else rows + term
        rank = ranks[...]
        for k in range(RANKS):
            part = slice(8 * k, 8 * k + 8)
            out_ref[part, :] = jnp.where(rank == float(k), rows[part], 0.0)
        for copy in self.sends:
            copy.wait_send()


CORNERS = ((-1, -1), (-1, 1), (1, -1), (1, 1))
SIDES = ((-1, 0), (1, 0), (0, -1), (0, 1))
GROUPS = CORNERS + SIDES + ((0, 0),)
BANDS = 5
STEP = 64
OUTS = BANDS + 6


def compute(
    side, src_ref, sky_ref, copy_in, out_ref,
    counts, weights, turned, prof_i, prof_j, low_i, low_j, scaled,
    rim_top, rim_bottom, rim_left, rim_right, sums,
):
    for b in range(BANDS):
        copy_in(b).wait()
    index = {group: n for n, group in enumerate(GROUPS)}

    def source(group, k, row):
        dr, dc = group
        start = (dc + 1) * 8 * RANKS + k * 8 + row
        return src_ref[dr + 1, start : start + 1, :]

    def span(step):
        if step == 0:
            return 0, side
        return (0, EDGE) if step < 0 else (side - EDGE, EDGE)

    def make_profile(group, axis, f32_ref, low_ref, scaled_ref):
        first, count = span(group[axis])
        base = first + 0.5 - group[axis] * side
        iota = lax.broadcasted_iota(jnp.int32, (STEP, LANES), 0).astype(F32)
        for k in range(RANKS):
            lanes = slice(k * LANES, (k + 1) * LANES)
            center = source(group, k, 5 + axis)
            inverse = 1.0 / (float(EDGE) * jnp.exp(source(group, k, 7)))
            factor = -HALF_LOG2E * inverse * inverse
            norm = inverse * (1.0 / ROOT_2PI)
            flux = [source(group, k, b) for b in range(BANDS)] if scaled_ref is not None else []

            def body(step, carry):
                start = pl.multiple_of(step * STEP, STEP)
                off = iota + (base + start.astype(F32)) - center
                prof = jnp.exp2(off * factor * off) * norm
                rows = pl.ds(start, STEP)
                f32_ref[rows, lanes] = prof
                if low_ref is not None:
                    low_ref[rows, lanes] = prof.astype(BF16)
                for b, f in enumerate(flux):
                    into = pl.ds(pl.multiple_of(b * count + step * STEP, STEP), STEP)
                    scaled_ref[into, lanes] = (prof * f).astype(BF16)
                return carry

            lax.fori_loop(0, count // STEP, body, 0, unroll=True)

    def rounded(x):
        return x.astype(BF16).astype(F32)

    class Pipeline:
        def __init__(self):
            self.held = None

        def add(self, product, consume):
            value = product()
            self.flush()
            self.held = functools.partial(consume, value)

        def flush(self):
            if self.held is not None:
                self.held()
            self.held = None

    line = Pipeline()
    rims_ij = {-1: rim_top, 1: rim_bottom}
    rims_ji = {-1: rim_left, 1: rim_right}
    own = index[(0, 0)]

    def profiles(group):
        n = index[group]
        by_row = group[0] or not group[1]
        make_profile(group, 0, prof_i[n], None if group[0] else low_i[n], scaled[n] if by_row else None)
        make_profile(group, 1, prof_j[n], low_j[n] if by_row else None, None if by_row else scaled[n])

    def render(group):
        n = index[group]
        if group[0] or not group[1]:
            return dot_tt(scaled[n][...], low_j[n][...])
        return dot_tt(low_i[n][...], scaled[n][...])

    def add_rim(group, model):
        dr, dc = group
        if dr:
            part = rounded(model).reshape(BANDS, EDGE, model.shape[1])
            if dc == 0:
                rims_ij[dr][...] = part
            else:
                start = 0 if dc < 0 else side - EDGE
                rims_ij[dr][:, :, start : start + EDGE] += part
        else:
            rims_ji[dc][...] = rounded(model)

    around = SIDES + CORNERS
    profiles(around[0])
    for here, following in zip(around, around[1:] + ((0, 0),)):
        profiles(following)
        line.add(functools.partial(render, here), functools.partial(add_rim, here))

    def own_model(b):
        return dot_tt(scaled[own][b * side : (b + 1) * side, :], low_j[own][...])

    def weigh(b, model):
        level = sky_ref[0, 0:1, b : b + 1]
        for chunk in range(side // EDGE):
            rows = slice(chunk * EDGE, (chunk + 1) * EDGE)
            for other in range(side // EDGE):
                cols = slice(other * EDGE, (other + 1) * EDGE)
                part = rounded(model[rows, cols]) + level
                if other == 0:
                    part = part + rim_left[rows, b * EDGE : (b + 1) * EDGE]
                if other == side // EDGE - 1:
                    part = part + rim_right[rows, b * EDGE : (b + 1) * EDGE]
                if chunk == 0:
                    part = part + rim_top[b, :, cols]
                if chunk == side // EDGE - 1:
                    part = part + rim_bottom[b, :, cols]
                ratio = counts[b, rows, cols].astype(F32) / part - 1.0
                low = ratio.astype(BF16)
                weights[b, rows, cols] = low
                turned[cols, b * side + chunk * EDGE : b * side + (chunk + 1) * EDGE] = low.T

    for b in range(BANDS):
        line.add(functools.partial(own_model, b), functools.partial(weigh, b))
    line.flush()

    def fold(x):
        return jnp.sum(x.reshape(x.shape[0] // 8, 8, x.shape[1]), axis=0)

    def put(n, k, at, value, add):
        if add:
            sums[n, k, at] += value
        else:
            sums[n, k, at] = value

    def moments(group, axis, k, start, total, prof, base, add):
        n = index[group]
        iota = lax.broadcasted_iota(jnp.int32, (8, LANES), 0).astype(F32)
        zeroth = first = second = None
        for run in range(total.shape[0] // EDGE):
            s0 = s1 = s2 = None
            for row in range(run * EDGE, (run + 1) * EDGE, 8):
                term = prof[row : row + 8] * total[row : row + 8]
                s0 = term if s0 is None else s0 + term
                s1 = s0 if s1 is None else s1 + s0
                s2 = s1 if s2 is None else s2 + s1
            end = iota + (base + (start + (run + 1) * EDGE)) - source(group, k, 5 + axis)
            scaled0 = end * s0
            one = scaled0 - 8.0 * s1
            two = end * (scaled0 - 16.0 * s1) + 64.0 * (s2 + (s2 - s1))
            zeroth = s0 if zeroth is None else zeroth + s0
            first = one if first is None else first + one
            second = two if second is None else second + two
        at = BANDS + 3 * axis
        put(n, k, at, zeroth, add)
        put(n, k, at + 1, first, add)
        put(n, k, at + 2, second, add)

    def per_band(group, axis, lhs, rhs, prof_ref, start, add):
        n = index[group]
        base = span(group[axis])[0] + 0.5 - group[axis] * side

        def consume(pair, along):
            for k in (2 * pair, 2 * pair + 1):
                lanes = slice((k - 2 * pair) * LANES, (k - 2 * pair + 1) * LANES)
                prof = prof_ref[start : start + EDGE, k * LANES : (k + 1) * LANES]
                low = rounded(prof)
                total = None
                for b in range(BANDS):
                    band = along[b * EDGE : (b + 1) * EDGE, lanes]
                    put(n, k, b, fold(low * band), add)
                    term = source(group, k, b) * band
                    total = term if total is None else total + term
                moments(group, axis, k, start, total, prof, base, add)

        for pair in range(RANKS // 2):
            wide = slice(pair * 2 * LANES, (pair + 1) * 2 * LANES)
            line.add(
                lambda wide=wide: dot_nn(lhs(), rhs[:, wide]), functools.partial(consume, pair)
            )

    def all_bands(group, axis, lhs, scaled_ref, prof_ref):
        base = span(group[axis])[0] + 0.5 - group[axis] * side

        def consume(pair, along):
            for k in (2 * pair, 2 * pair + 1):
                lanes = slice((k - 2 * pair) * LANES, (k - 2 * pair + 1) * LANES)
                prof = prof_ref[:, k * LANES : (k + 1) * LANES]
                moments(group, axis, k, 0, along[:, lanes], prof, base, False)

        for pair in range(RANKS // 2):
            wide = slice(pair * 2 * LANES, (pair + 1) * 2 * LANES)
            line.add(
                lambda wide=wide: dot_nn(lhs(), scaled_ref[:, wide]),
                functools.partial(consume, pair),
            )

    def near_rows(group):
        (r0, rn), (c0, cn) = span(group[0]), span(group[1])
        return weights[:, r0 : r0 + rn, c0 : c0 + cn].reshape(BANDS * rn, cn)

    def far_cols(group):
        (r0, rn), (c0, cn) = span(group[0]), span(group[1])
        at = [b * side + r0 for b in range(BANDS)]
        return jnp.concatenate([turned[c0 : c0 + cn, r : r + rn] for r in at], axis=1)

    def near_cols(group):
        c0, cn = span(group[1])
        at = [b * side for b in range(BANDS)]
        return jnp.concatenate([turned[c0 : c0 + cn, r : r + side] for r in at], axis=0)

    def far_rows(group):
        c0, cn = span(group[1])
        return jnp.concatenate([weights[b, :, c0 : c0 + cn] for b in range(BANDS)], axis=1)

    def side_grads(group):
        n = index[group]
        if group[0]:
            lhs = functools.partial(near_rows, group)
            per_band(group, 0, lhs, low_j[n], prof_i[n], 0, False)
            all_bands(group, 1, functools.partial(far_cols, group), scaled[n], prof_j[n])
        else:
            lhs = functools.partial(near_cols, group)
            per_band(group, 1, lhs, low_i[n], prof_j[n], 0, False)
            all_bands(group, 0, functools.partial(far_rows, group), scaled[n], prof_i[n])

    def own_rows(start):
        return weights[:, start : start + EDGE, :].reshape(BANDS * EDGE, side)

    def own_grads():
        for start in range(0, side, EDGE):
            lhs = functools.partial(own_rows, start)
            per_band((0, 0), 0, lhs, low_j[own], prof_i[own], start, start > 0)
        all_bands((0, 0), 1, lambda: turned[...], scaled[own], prof_j[own])

    def collect(group):
        n, (dr, dc) = index[group], group
        for k in range(RANKS):
            inverse = 1.0 / (float(EDGE) * jnp.exp(source(group, k, 7)))
            square = inverse * inverse

            def total(which):
                return jnp.sum(sums[n, k, which], axis=0, keepdims=True)

            start = (dc + 1) * 8 * RANKS + k * 8
            for b in range(BANDS):
                out_ref[dr + 1, start + b : start + b + 1, :] = source(group, k, b) * total(b)
            zeroth = total(BANDS) + total(BANDS + 3)
            second = total(BANDS + 2) + total(BANDS + 5)
            out_ref[dr + 1, start + 5 : start + 6, :] = total(BANDS + 1) * square
            out_ref[dr + 1, start + 6 : start + 7, :] = total(BANDS + 4) * square
            out_ref[dr + 1, start + 7 : start + 8, :] = second * square - zeroth

    for step in (-1, 1, 0):
        groups = [group for group in around if group[0] == step]
        for group in groups:
            side_grads(group)
        if step == 0:
            own_grads()
            groups.append((0, 0))

    line.flush()
    out_ref[...] = jnp.zeros(out_ref.shape, F32)
    for group in GROUPS:
        collect(group)


def fused_kernel(
    na, nd, side, flux_ref, pos_ref, width_ref, tile_ref, sky_ref, counts_ref, out_ref,
    counts, count_sem, sky, flux, position, width, tiles, input_sem, onehot, ranks,
    sources, partial, to_route, to_compute, to_return,
):
    place = Place(na, nd)
    greet(place)
    fetched = [
        pltpu.make_async_copy(src, dst, input_sem.at[n])
        for n, (src, dst) in enumerate(
            [
                (tile_ref, tiles), (flux_ref, flux), (pos_ref, position),
                (width_ref, width), (sky_ref, sky),
            ]
        )
    ]
    for copy in fetched:
        copy.start()

    def copy_in(b):
        return pltpu.make_async_copy(counts_ref.at[b], counts.at[b], count_sem.at[b])

    for b in range(BANDS):
        copy_in(b).start()
    params, *rest = to_route
    sends = route(
        na, nd, place, fetched, sources, flux, position, width, tiles, params, onehot, ranks, *rest
    )
    back = GiveBack(place, partial, *to_return)
    compute(side, sources, sky, copy_in, partial, counts, *to_compute)
    back.finish(onehot, ranks, out_ref)
    for copy in sends:
        copy.wait_send()


def buffer(*shape, dtype=F32):
    return pltpu.VMEM(shape, dtype)


def compute_buffers(side):
    slots = RANKS * LANES
    spare = 16

    def extent(step):
        return EDGE if step else side

    return [
        buffer(BANDS, side, side, dtype=BF16),
        buffer(side, BANDS * side, dtype=BF16),
        [buffer(extent(g[0]), slots) for g in GROUPS],
        [buffer(extent(g[1]), slots) for g in GROUPS],
        [buffer(spare if g[0] else side, slots, dtype=BF16) for g in GROUPS],
        [
            buffer(extent(g[1]) if g[0] or not g[1] else spare, slots, dtype=BF16)
            for g in GROUPS
        ],
        [buffer(BANDS * (EDGE if any(g) else side), slots, dtype=BF16) for g in GROUPS],
        buffer(BANDS, EDGE, side),
        buffer(BANDS, EDGE, side),
        buffer(side, BANDS * EDGE),
        buffer(side, BANDS * EDGE),
        buffer(len(GROUPS), RANKS, OUTS, 8, LANES),
    ]


def on_device(na, nd, log_flux, position, log_width, owner_tile, sky_level, counts):
    rows = log_flux.shape[1]
    side = counts.shape[1]
    width = log_width.reshape(1, rows)
    tile = owner_tile.reshape(1, rows)
    dma = pltpu.SemaphoreType.DMA
    near = 8
    far = na * nd // near

    masked = pl.pallas_call(
        functools.partial(fused_kernel, na, nd, side),
        out_shape=jax.ShapeDtypeStruct((RANKS * 8, rows), F32),
        in_specs=[pl.BlockSpec(memory_space=pl.ANY)] * 6,
        out_specs=VMEM,
        scratch_shapes=[
            buffer(BANDS, side, side, dtype=jnp.int32),
            dma((BANDS,)),
            buffer(*sky_level.shape),
            buffer(*log_flux.shape),
            buffer(*position.shape),
            buffer(1, rows),
            buffer(1, rows, dtype=jnp.int32),
            dma((5,)),
            buffer(SIDE_REACH, LANES, rows, dtype=BF16),
            buffer(1, rows),
            buffer(3, LANES, na * nd),
            buffer(3, LANES, na * nd),
            [
                buffer(8, rows),
                buffer(far, 8, LANES),
                buffer(far, 8, LANES),
                buffer(REACH, far, LANES),
                buffer(near, 3, far, LANES),
                dma((far,)), dma((far,)), dma((near,)), dma((near,)),
            ],
            compute_buffers(side),
            [
                buffer(near, 3, far, LANES),
                buffer(near, 3, far, LANES),
                buffer(far, 8, LANES),
                buffer(far, 8, LANES),
                dma((near,)), dma((near,)), dma((far,)), dma((far,)),
            ],
        ],
        compiler_params=pltpu.CompilerParams(
            collective_id=0, has_side_effects=True, vmem_limit_bytes=60 << 20
        ),
        name="fused",
    )(log_flux, position, width, tile, sky_level, counts)
    return jnp.sum(masked.reshape(RANKS, 8, rows), axis=0)


def solution(mesh):
    na, nd = mesh.shape["ra"], mesh.shape["dec"]
    in_specs = (
        P(None, ("ra", "dec")),
        P(None, ("ra", "dec")),
        P(("ra", "dec")),
        P(("ra", "dec"), None),
        P("ra", "dec", None),
        P(None, "ra", "dec"),
    )
    return jax.shard_map(
        functools.partial(on_device, na, nd),
        mesh=mesh,
        in_specs=in_specs,
        out_specs=P(None, ("ra", "dec")),
        check_vma=False,
    )
```

```python
import functools
import math

import jax
import jax.numpy as jnp
from jax import lax
from jax.experimental import pallas as pl
from jax.experimental.pallas import tpu as pltpu
from jax.sharding import PartitionSpec as P

F32 = jnp.float32
BF16 = jnp.bfloat16
MESH = pl.DeviceIdType.MESH
VMEM = pl.BlockSpec(memory_space=pltpu.VMEM)

EDGE = 128
RANKS = 4
LANES = 128
HALF_LOG2E = 0.5 * math.log2(math.e)
ROOT_2PI = math.sqrt(2.0 * math.pi)


def split3(x):
    hi = x.astype(BF16)
    rest = x - hi.astype(F32)
    mid = rest.astype(BF16)
    lo = (rest - mid.astype(F32)).astype(BF16)
    return hi, mid, lo


def dot_tt(a, b):
    return lax.dot_general(a, b, (((1,), (1,)), ((), ())), preferred_element_type=F32)


def dot_nn(a, b):
    return lax.dot_general(a, b, (((1,), (0,)), ((), ())), preferred_element_type=F32)


def ranks_of(tile):
    rows = tile.shape[1]
    names = lax.broadcasted_iota(jnp.int32, (LANES, rows), 0)
    onehot = names == tile
    earlier = lax.broadcasted_iota(jnp.int32, (rows, rows), 0) < lax.broadcasted_iota(
        jnp.int32, (rows, rows), 1
    )
    before = dot_nn(
        jnp.where(onehot, 1.0, 0.0).astype(BF16), jnp.where(earlier, 1.0, 0.0).astype(BF16)
    )
    rank = jnp.sum(jnp.where(onehot, before, 0.0), axis=0, keepdims=True)
    return names, rank


class Place:
    def __init__(self, na, nd):
        ring_x, ring_z = na // 4, nd // 2
        a, d = lax.axis_index("ra"), lax.axis_index("dec")
        x, h, k, z, low = a // 4, lax.rem(a // 2, 2), lax.rem(a, 2), d // 2, lax.rem(d, 2)
        self.far_count, self.near_count, self.ring_z = ring_x * ring_z, 8, ring_z
        self.low, self.far_here, self.near_here = low, x * ring_z + z, h * 4 + k * 2 + low
        steps = [(i, j) for i in range(ring_x) for j in range(ring_z)][1:]
        steps.sort(key=lambda o: -(min(o[0], ring_x - o[0]) + min(o[1], ring_z - o[1])))
        self.far = []
        for i, j in steps:
            px, pz = lax.rem(x + i, ring_x), lax.rem(z + j, ring_z)
            self.far.append((px * 4 + h * 2 + k, pz * 2 + low, px * ring_z + pz))
        turns = [(i, j, m) for i in range(2) for j in range(2) for m in range(2)][1:]
        turns.sort(key=lambda o: -(4 * o[0] - 2 * o[0] * o[2] + 2 * o[2] + o[1]))
        self.near = []
        for i, j, m in turns:
            ph, pk, pl_ = lax.rem(h + i, 2), lax.rem(k + j, 2), lax.rem(low + m, 2)
            self.near.append((x * 4 + ph * 2 + pk, z * 2 + pl_, ph * 4 + pk * 2 + pl_))


REACH = 6
SIDE_REACH = 4


def reached(na, nd, ring_z, column, rows):
    number = lax.broadcasted_iota(jnp.int32, (LANES, rows), 0)
    bits = ring_z.bit_length() - 1
    step = number & 7
    a = lax.shift_right_logical(number, 3 + bits) * 4 - 1 + step
    d = (lax.shift_right_logical(number, 3) & (ring_z - 1)) * 2 - 1 + column
    known = (step < REACH) & (a >= 0) & (a < na) & (d >= 0) & (d < nd)
    return jnp.where(known, a * nd + d, -1)


def send(src, dst, send_sem, recv_sem, a, d):
    return pltpu.make_async_remote_copy(
        src_ref=src, dst_ref=dst, send_sem=send_sem, recv_sem=recv_sem,
        device_id=(a, d), device_id_type=MESH,
    )


def greet(place):
    barrier = pltpu.get_barrier_semaphore()
    for a, d, _ in place.far + place.near:
        pl.semaphore_signal(barrier, inc=1, device_id=(a, d), device_id_type=MESH)


def route(
    na, nd, place, fetched, out_ref,
    flux, position, width, tiles, params, onehot, ranks, first, got1, stage, got2,
    send1, recv1, send2, recv2,
):
    for copy in fetched:
        copy.wait()
    params[0:5, :] = jnp.exp(flux[...])
    params[5:7, :] = position[...]
    params[7:8, :] = width[...]
    tile = tiles[...]
    rows = tile.shape[1]
    _, rank = ranks_of(tile)
    ranks[...] = rank
    block = params[...]
    ranked = jnp.concatenate(
        [jnp.where(rank == float(k), block, 0.0) for k in range(RANKS)], axis=0
    )
    none = jnp.zeros(ranked.shape, BF16)
    pieces = split3(ranked)
    total = None
    for n in range(SIDE_REACH):
        names = reached(na, nd, place.ring_z, n, rows)
        hot = jnp.where(names == tile, 1.0, 0.0).astype(BF16)
        onehot[n] = hot
        for piece in pieces:
            rhs = jnp.concatenate([piece if m == n else none for m in range(SIDE_REACH)], axis=0)
            term = dot_tt(hot, rhs)
            total = term if total is None else total + term
    first[...] = total.reshape(first.shape)
    pl.semaphore_wait(pltpu.get_barrier_semaphore(), len(place.far) + len(place.near))

    sends = []
    here = place.far_here
    for i, (a, d, peer) in enumerate(place.far):
        copy = send(first.at[peer], got1.at[here], send1.at[i], recv1.at[here], a, d)
        copy.start()
        sends.append(copy)
    got1[here] = first[here]
    for i, (a, d, peer) in enumerate(place.far):
        send(first.at[peer], got1.at[peer], send1.at[i], recv1.at[peer], a, d).wait_recv()
    for step in range(REACH):
        stage[step] = got1[:, step, :]
    here = place.near_here
    for i, (a, d, peer) in enumerate(place.near):
        part = stage.at[pl.ds(peer // 2, 3)]
        copy = send(part, got2.at[here], send2.at[i], recv2.at[here], a, d)
        copy.start()
        sends.append(copy)
    got2[here] = stage[pl.ds(here // 2, 3)]
    for i, (a, d, peer) in enumerate(place.near):
        part = stage.at[pl.ds(peer // 2, 3)]
        send(part, got2.at[peer], send2.at[i], recv2.at[peer], a, d).wait_recv()
    for n in range(3):
        turned = got2[:, n].reshape(LANES, LANES).T
        out_ref[n] = jnp.where(place.low == 1, pltpu.roll(turned, LANES - 8 * RANKS, 0), turned)
    return sends


class GiveBack:
    def __init__(self, place, grad_ref, first, got1, stage, got2, send1, recv1, send2, recv2):
        self.place, self.grad_ref = place, grad_ref
        self.first, self.got1, self.stage, self.got2 = first, got1, stage, got2
        self.send1, self.recv1, self.send2, self.recv2 = send1, recv1, send2, recv2
        self.sends = []
        stage[...] = jnp.zeros_like(stage)

    def to_near(self, i, number):
        a, d, peer = self.place.near[i]
        return send(
            self.first.at[peer], self.got1.at[number], self.send1.at[i], self.recv1.at[number], a, d
        )

    def finish(self, onehot, ranks, out_ref):
        place, got1, stage, got2 = self.place, self.got1, self.stage, self.got2
        for n in range(3):
            grads = self.grad_ref[n]
            grads = jnp.where(place.low == 1, pltpu.roll(grads, 8 * RANKS, 0), grads)
            self.first[:, n] = grads.T.reshape(place.near_count, place.far_count, LANES)
        for i in range(len(place.near)):
            copy = self.to_near(i, place.near_here)
            copy.start()
            self.sends.append(copy)
        got1[place.near_here] = self.first[place.near_here]
        for i, (_, _, peer) in enumerate(place.near):
            self.to_near(i, peer).wait_recv()
        for step in range(REACH):
            part = None
            for n in range(3):
                for number in range(place.near_count):
                    if number // 2 + n == step:
                        part = got1[number, n] if part is None else part + got1[number, n]
            stage[:, step, :] = part
        here = place.far_here
        for i, (a, d, peer) in enumerate(place.far):
            copy = send(
                stage.at[peer], got2.at[here], self.send2.at[i], self.recv2.at[here], a, d
            )
            copy.start()
            self.sends.append(copy)
        got2[here] = stage[here]
        for i, (a, d, peer) in enumerate(place.far):
            send(
                stage.at[peer], got2.at[peer], self.send2.at[i], self.recv2.at[peer], a, d
            ).wait_recv()
        held, width = got2[...].reshape(LANES, LANES).T, 8 * RANKS
        rows = None
        for n in range(SIDE_REACH):
            for piece in split3(held[n * width : (n + 1) * width]):
                term = dot_nn(piece, onehot[n])
                rows = term if rows is None else rows + term
        rank = ranks[...]
        for k in range(RANKS):
            part = slice(8 * k, 8 * k + 8)
            out_ref[part, :] = jnp.where(rank == float(k), rows[part], 0.0)
        for copy in self.sends:
            copy.wait_send()


CORNERS = ((-1, -1), (-1, 1), (1, -1), (1, 1))
SIDES = ((-1, 0), (1, 0), (0, -1), (0, 1))
GROUPS = CORNERS + SIDES + ((0, 0),)
BANDS = 5
STEP = 64
OUTS = BANDS + 6


def compute(
    side, src_ref, sky_ref, copy_in, out_ref,
    counts, weights, turned, prof_i, prof_j, low_i, low_j, scaled,
    rim_top, rim_bottom, rim_left, rim_right, sums,
):
    for b in range(BANDS):
        copy_in(b).wait()
    index = {group: n for n, group in enumerate(GROUPS)}

    def source(group, k, row):
        dr, dc = group
        start = (dc + 1) * 8 * RANKS + k * 8 + row
        return src_ref[dr + 1, start : start + 1, :]

    def span(step):
        if step == 0:
            return 0, side
        return (0, EDGE) if step < 0 else (side - EDGE, EDGE)

    def make_profile(group, axis, f32_ref, low_ref, scaled_ref):
        first, count = span(group[axis])
        base = first + 0.5 - group[axis] * side
        iota = lax.broadcasted_iota(jnp.int32, (STEP, LANES), 0).astype(F32)
        for k in range(RANKS):
            lanes = slice(k * LANES, (k + 1) * LANES)
            center = source(group, k, 5 + axis)
            inverse = 1.0 / (float(EDGE) * jnp.exp(source(group, k, 7)))
            factor = -HALF_LOG2E * inverse * inverse
            norm = inverse * (1.0 / ROOT_2PI)
            flux = [source(group, k, b) for b in range(BANDS)] if scaled_ref is not None else []

            def body(step, carry):
                start = pl.multiple_of(step * STEP, STEP)
                off = iota + (base + start.astype(F32)) - center
                prof = jnp.exp2(off * factor * off) * norm
                rows = pl.ds(start, STEP)
                f32_ref[rows, lanes] = prof
                if low_ref is not None:
                    low_ref[rows, lanes] = prof.astype(BF16)
                for b, f in enumerate(flux):
                    into = pl.ds(pl.multiple_of(b * count + step * STEP, STEP), STEP)
                    scaled_ref[into, lanes] = (prof * f).astype(BF16)
                return carry

            lax.fori_loop(0, count // STEP, body, 0, unroll=True)

    def rounded(x):
        return x.astype(BF16).astype(F32)

    class Pipeline:
        def __init__(self):
            self.held = None

        def add(self, product, consume):
            value = product()
            self.flush()
            self.held = functools.partial(consume, value)

        def flush(self):
            if self.held is not None:
                self.held()
            self.held = None

    line = Pipeline()
    rims_ij = {-1: rim_top, 1: rim_bottom}
    rims_ji = {-1: rim_left, 1: rim_right}
    own = index[(0, 0)]

    def profiles(group):
        n = index[group]
        by_row = group[0] or not group[1]
        make_profile(group, 0, prof_i[n], None if group[0] else low_i[n], scaled[n] if by_row else None)
        make_profile(group, 1, prof_j[n], low_j[n] if by_row else None, None if by_row else scaled[n])

    def render(group):
        n = index[group]
        if group[0] or not group[1]:
            return dot_tt(scaled[n][...], low_j[n][...])
        return dot_tt(low_i[n][...], scaled[n][...])

    def add_rim(group, model):
        dr, dc = group
        if dr:
            part = rounded(model).reshape(BANDS, EDGE, model.shape[1])
            if dc == 0:
                rims_ij[dr][...] = part
            else:
                start = 0 if dc < 0 else side - EDGE
                rims_ij[dr][:, :, start : start + EDGE] += part
        else:
            rims_ji[dc][...] = rounded(model)

    around = SIDES + CORNERS
    profiles(around[0])
    for here, following in zip(around, around[1:] + ((0, 0),)):
        profiles(following)
        line.add(functools.partial(render, here), functools.partial(add_rim, here))

    def own_model(b):
        return dot_tt(scaled[own][b * side : (b + 1) * side, :], low_j[own][...])

    def weigh(b, model):
        level = sky_ref[0, 0:1, b : b + 1]
        for chunk in range(side // EDGE):
            rows = slice(chunk * EDGE, (chunk + 1) * EDGE)
            for other in range(side // EDGE):
                cols = slice(other * EDGE, (other + 1) * EDGE)
                part = rounded(model[rows, cols]) + level
                if other == 0:
                    part = part + rim_left[rows, b * EDGE : (b + 1) * EDGE]
                if other == side // EDGE - 1:
                    part = part + rim_right[rows, b * EDGE : (b + 1) * EDGE]
                if chunk == 0:
                    part = part + rim_top[b, :, cols]
                if chunk == side // EDGE - 1:
                    part = part + rim_bottom[b, :, cols]
                ratio = counts[b, rows, cols].astype(F32) / part - 1.0
                low = ratio.astype(BF16)
                weights[b, rows, cols] = low
                turned[cols, b * side + chunk * EDGE : b * side + (chunk + 1) * EDGE] = low.T

    for b in range(BANDS):
        line.add(functools.partial(own_model, b), functools.partial(weigh, b))
    most = (BANDS - 1) * side
    begun = [
        dot_nn(turned[:, :most], scaled[own][:most, n * 2 * LANES : (n + 1) * 2 * LANES])
        for n in range(RANKS // 2)
    ]
    line.flush()

    def fold(x):
        return jnp.sum(x.reshape(x.shape[0] // 8, 8, x.shape[1]), axis=0)

    def put(n, k, at, value, add):
        if add:
            sums[n, k, at] += value
        else:
            sums[n, k, at] = value

    def moments(group, axis, k, start, total, prof, base, add):
        n = index[group]
        iota = lax.broadcasted_iota(jnp.int32, (8, LANES), 0).astype(F32)
        zeroth = first = second = None
        for run in range(total.shape[0] // EDGE):
            s0 = s1 = s2 = None
            for row in range(run * EDGE, (run + 1) * EDGE, 8):
                term = prof[row : row + 8] * total[row : row + 8]
                s0 = term if s0 is None else s0 + term
                s1 = s0 if s1 is None else s1 + s0
                s2 = s1 if s2 is None else s2 + s1
            end = iota + (base + (start + (run + 1) * EDGE)) - source(group, k, 5 + axis)
            scaled0 = end * s0
            one = scaled0 - 8.0 * s1
            two = end * (scaled0 - 16.0 * s1) + 64.0 * (s2 + (s2 - s1))
            zeroth = s0 if zeroth is None else zeroth + s0
            first = one if first is None else first + one
            second = two if second is None else second + two
        at = BANDS + 3 * axis
        put(n, k, at, zeroth, add)
        put(n, k, at + 1, first, add)
        put(n, k, at + 2, second, add)

    def per_band(group, axis, lhs, rhs, prof_ref, start, add):
        n = index[group]
        base = span(group[axis])[0] + 0.5 - group[axis] * side

        def consume(pair, along):
            for k in (2 * pair, 2 * pair + 1):
                lanes = slice((k - 2 * pair) * LANES, (k - 2 * pair + 1) * LANES)
                prof = prof_ref[start : start + EDGE, k * LANES : (k + 1) * LANES]
                low = rounded(prof)
                total = None
                for b in range(BANDS):
                    band = along[b * EDGE : (b + 1) * EDGE, lanes]
                    put(n, k, b, fold(low * band), add)
                    term = source(group, k, b) * band
                    total = term if total is None else total + term
                moments(group, axis, k, start, total, prof, base, add)

        for pair in range(RANKS // 2):
            wide = slice(pair * 2 * LANES, (pair + 1) * 2 * LANES)
            line.add(
                lambda wide=wide: dot_nn(lhs(), rhs[:, wide]), functools.partial(consume, pair)
            )

    def all_bands(group, axis, lhs, scaled_ref, prof_ref, begun=None):
        base = span(group[axis])[0] + 0.5 - group[axis] * side

        def consume(pair, along):
            if begun is not None:
                along = begun[pair] + along
            for k in (2 * pair, 2 * pair + 1):
                lanes = slice((k - 2 * pair) * LANES, (k - 2 * pair + 1) * LANES)
                prof = prof_ref[:, k * LANES : (k + 1) * LANES]
                moments(group, axis, k, 0, along[:, lanes], prof, base, False)

        for pair in range(RANKS // 2):
            wide = slice(pair * 2 * LANES, (pair + 1) * 2 * LANES)
            line.add(
                lambda wide=wide: dot_nn(lhs(), scaled_ref[:, wide]),
                functools.partial(consume, pair),
            )

    def near_rows(group):
        (r0, rn), (c0, cn) = span(group[0]), span(group[1])
        return weights[:, r0 : r0 + rn, c0 : c0 + cn].reshape(BANDS * rn, cn)

    def far_cols(group):
        (r0, rn), (c0, cn) = span(group[0]), span(group[1])
        at = [b * side + r0 for b in range(BANDS)]
        return jnp.concatenate([turned[c0 : c0 + cn, r : r + rn] for r in at], axis=1)

    def near_cols(group):
        c0, cn = span(group[1])
        at = [b * side for b in range(BANDS)]
        return jnp.concatenate([turned[c0 : c0 + cn, r : r + side] for r in at], axis=0)

    def far_rows(group):
        c0, cn = span(group[1])
        return jnp.concatenate([weights[b, :, c0 : c0 + cn] for b in range(BANDS)], axis=1)

    def side_grads(group):
        n = index[group]
        if group[0]:
            lhs = functools.partial(near_rows, group)
            per_band(group, 0, lhs, low_j[n], prof_i[n], 0, False)
            all_bands(group, 1, functools.partial(far_cols, group), scaled[n], prof_j[n])
        else:
            lhs = functools.partial(near_cols, group)
            per_band(group, 1, lhs, low_i[n], prof_j[n], 0, False)
            all_bands(group, 0, functools.partial(far_rows, group), scaled[n], prof_i[n])

    def own_rows(start):
        return weights[:, start : start + EDGE, :].reshape(BANDS * EDGE, side)

    def own_grads():
        for start in range(0, side, EDGE):
            lhs = functools.partial(own_rows, start)
            per_band((0, 0), 0, lhs, low_j[own], prof_i[own], start, start > 0)
        last = scaled[own].at[most : most + side]
        all_bands((0, 0), 1, lambda: turned[:, most:], last, prof_j[own], begun)

    def collect(group):
        n, (dr, dc) = index[group], group
        for k in range(RANKS):
            inverse = 1.0 / (float(EDGE) * jnp.exp(source(group, k, 7)))
            square = inverse * inverse

            def total(which):
                return jnp.sum(sums[n, k, which], axis=0, keepdims=True)

            start = (dc + 1) * 8 * RANKS + k * 8
            for b in range(BANDS):
                out_ref[dr + 1, start + b : start + b + 1, :] = source(group, k, b) * total(b)
            zeroth = total(BANDS) + total(BANDS + 3)
            second = total(BANDS + 2) + total(BANDS + 5)
            out_ref[dr + 1, start + 5 : start + 6, :] = total(BANDS + 1) * square
            out_ref[dr + 1, start + 6 : start + 7, :] = total(BANDS + 4) * square
            out_ref[dr + 1, start + 7 : start + 8, :] = second * square - zeroth

    for step in (-1, 1, 0):
        groups = [group for group in around if group[0] == step]
        for group in groups:
            side_grads(group)
        if step == 0:
            own_grads()
            groups.append((0, 0))

    line.flush()
    out_ref[...] = jnp.zeros(out_ref.shape, F32)
    for group in GROUPS:
        collect(group)


def fused_kernel(
    na, nd, side, flux_ref, pos_ref, width_ref, tile_ref, sky_ref, counts_ref, out_ref,
    counts, count_sem, sky, flux, position, width, tiles, input_sem, onehot, ranks,
    sources, partial, to_route, to_compute, to_return,
):
    place = Place(na, nd)
    greet(place)
    fetched = [
        pltpu.make_async_copy(src, dst, input_sem.at[n])
        for n, (src, dst) in enumerate(
            [
                (tile_ref, tiles), (flux_ref, flux), (pos_ref, position),
                (width_ref, width), (sky_ref, sky),
            ]
        )
    ]
    for copy in fetched:
        copy.start()

    def copy_in(b):
        return pltpu.make_async_copy(counts_ref.at[b], counts.at[b], count_sem.at[b])

    for b in range(BANDS):
        copy_in(b).start()
    params, *rest = to_route
    sends = route(
        na, nd, place, fetched, sources, flux, position, width, tiles, params, onehot, ranks, *rest
    )
    back = GiveBack(place, partial, *to_return)
    compute(side, sources, sky, copy_in, partial, counts, *to_compute)
    back.finish(onehot, ranks, out_ref)
    for copy in sends:
        copy.wait_send()


def buffer(*shape, dtype=F32):
    return pltpu.VMEM(shape, dtype)


def compute_buffers(side):
    slots = RANKS * LANES
    spare = 16

    def extent(step):
        return EDGE if step else side

    return [
        buffer(BANDS, side, side, dtype=BF16),
        buffer(side, BANDS * side, dtype=BF16),
        [buffer(extent(g[0]), slots) for g in GROUPS],
        [buffer(extent(g[1]), slots) for g in GROUPS],
        [buffer(spare if g[0] else side, slots, dtype=BF16) for g in GROUPS],
        [
            buffer(extent(g[1]) if g[0] or not g[1] else spare, slots, dtype=BF16)
            for g in GROUPS
        ],
        [buffer(BANDS * (EDGE if any(g) else side), slots, dtype=BF16) for g in GROUPS],
        buffer(BANDS, EDGE, side),
        buffer(BANDS, EDGE, side),
        buffer(side, BANDS * EDGE),
        buffer(side, BANDS * EDGE),
        buffer(len(GROUPS), RANKS, OUTS, 8, LANES),
    ]


def on_device(na, nd, log_flux, position, log_width, owner_tile, sky_level, counts):
    rows = log_flux.shape[1]
    side = counts.shape[1]
    width = log_width.reshape(1, rows)
    tile = owner_tile.reshape(1, rows)
    dma = pltpu.SemaphoreType.DMA
    near = 8
    far = na * nd // near

    masked = pl.pallas_call(
        functools.partial(fused_kernel, na, nd, side),
        out_shape=jax.ShapeDtypeStruct((RANKS * 8, rows), F32),
        in_specs=[pl.BlockSpec(memory_space=pl.ANY)] * 6,
        out_specs=VMEM,
        scratch_shapes=[
            buffer(BANDS, side, side, dtype=jnp.int32),
            dma((BANDS,)),
            buffer(*sky_level.shape),
            buffer(*log_flux.shape),
            buffer(*position.shape),
            buffer(1, rows),
            buffer(1, rows, dtype=jnp.int32),
            dma((5,)),
            buffer(SIDE_REACH, LANES, rows, dtype=BF16),
            buffer(1, rows),
            buffer(3, LANES, na * nd),
            buffer(3, LANES, na * nd),
            [
                buffer(8, rows),
                buffer(far, 8, LANES),
                buffer(far, 8, LANES),
                buffer(REACH, far, LANES),
                buffer(near, 3, far, LANES),
                dma((far,)), dma((far,)), dma((near,)), dma((near,)),
            ],
            compute_buffers(side),
            [
                buffer(near, 3, far, LANES),
                buffer(near, 3, far, LANES),
                buffer(far, 8, LANES),
                buffer(far, 8, LANES),
                dma((near,)), dma((near,)), dma((far,)), dma((far,)),
            ],
        ],
        compiler_params=pltpu.CompilerParams(
            collective_id=0, has_side_effects=True, vmem_limit_bytes=60 << 20
        ),
        name="fused",
    )(log_flux, position, width, tile, sky_level, counts)
    return jnp.sum(masked.reshape(RANKS, 8, rows), axis=0)


def solution(mesh):
    na, nd = mesh.shape["ra"], mesh.shape["dec"]
    in_specs = (
        P(None, ("ra", "dec")),
        P(None, ("ra", "dec")),
        P(("ra", "dec")),
        P(("ra", "dec"), None),
        P("ra", "dec", None),
        P(None, "ra", "dec"),
    )
    return jax.shard_map(
        functools.partial(on_device, na, nd),
        mesh=mesh,
        in_specs=in_specs,
        out_specs=P(None, ("ra", "dec")),
        check_vma=False,
    )
```
